32 devices in a mesh: grp: 4 (over z), term: 8 (over y, x, core).
Axes of the slice: x: 2, y: 2, z: 4, core: 2. Of those that a mesh axis runs over, the one named last changes fastest.
Arguments:
- hidden_states: bfloat16 [16384, 768], P(('grp', 'term')), may hold values from -8 to 8
- lengths: int32 [128], P(('grp', 'term')), may hold values from 32 to 128, as said below
- block_list: int32 [128, 96], P(('grp', 'term')), may hold values from 0 to 128, as said below
- cluster_ids: int32 [128], P(('grp', 'term')), may hold values from 0 to 16383, as said below
- attn_weight: bfloat16 [768, 2304], replicated, may hold values from -4 to 4
- out_weight: bfloat16 [768, 768], replicated, may hold values from -0.21875 to 0.21875
- up_weight: bfloat16 [768, 3072], replicated, may hold values from -0.21875 to 0.21875
- down_weight: bfloat16 [3072, 768], replicated, may hold values from -0.109375 to 0.109375
- head_weight: bfloat16 [768, 768], replicated, may hold values from -0.21875 to 0.21875
- head_gain: float32 [768], replicated, may hold values from 0.1 to 1.9
- vocab_weight: bfloat16 [16384, 768], P('term'), may hold values from -0.21875 to 0.21875
- vocab_bias: bfloat16 [16384], P('term'), may hold values from 0 to 2
- centroids: bfloat16 [16384, 768], P(('grp', 'term')), may hold values from -6 to 6
Outputs:
- sparse_weights: bfloat16 [128, 16384], P('grp', 'term')
- dense_slots: bfloat16 [32, 16, 768], P(('grp', 'term'))
- slot_passage: int32 [32, 16], P(('grp', 'term'))
The draws below stay inside these ranges and needn't reach their ends.
Inputs may be any that keep to these rules, and one draw needn't show every extreme that they name: `lengths`: the first token of every passage is live; some passage has all 128 tokens live. `block_list`: the live entries of a row are distinct term blocks and come first; the rest equal 128, which names no block. Every row has at least 48 live entries and at least one padding entry. The 4 passages of one device have distinct owners (cluster_ids // 512). No owner has more than 16 passages, and some owner has exactly 16.
All inputs are finite; a program needn't handle non-finite values.
Results may differ from the reference program's by a relative error of at most 0.007.
Values may be sent and summed in bfloat16 or wider, within the bound.
A program may use at most 128 MiB of HBM per device.

```python
import math
import jax
import jax.numpy as jnp
from jax import lax

D = 768
HEAD = 64
FF = 3072
VOCAB = 16384
BLOCK = 128
SEQ = 128
P_DEV = 4
NB = 96
CL_DEV = 512
CAP = 16
PASSAGES = 128
TOKENS = 16384
BLOCKS = 128
CLUSTERS = 16384
DEVICES = 32


def draw_hidden_states(key, part):
    values = jax.random.normal(key, (TOKENS, D), jnp.float32)
    return jnp.clip(values, -8.0, 8.0).astype(jnp.bfloat16)


def draw_attn_weight(key, part):
    values = jax.random.normal(key, (D, 3 * D), jnp.float32) / math.sqrt(D)
    return jnp.clip(values, -4.0, 4.0).astype(jnp.bfloat16)


def draw_lengths(key, part):
    drawn = jax.random.randint(key, (PASSAGES,), SEQ // 4, SEQ + 1)
    places = jnp.arange(PASSAGES, dtype=jnp.int32)
    drawn = jnp.where(places == 0, SEQ, drawn)
    drawn = jnp.where(places == 1, SEQ // 4, drawn)
    return drawn.astype(jnp.int32)


def draw_block_list(key, part):
    row_keys = jax.random.split(key, PASSAGES)
    chosen = jax.vmap(lambda row_key: jax.random.permutation(row_key, BLOCKS)[:NB])(row_keys)
    counts = jax.random.randint(jax.random.fold_in(key, 7), (PASSAGES, 1), NB // 2, NB)
    slots = jnp.arange(NB, dtype=jnp.int32)[None, :]
    return jnp.where(slots < counts, chosen, BLOCKS).astype(jnp.int32)


def draw_cluster_ids(key, part):
    mapping = jax.random.permutation(jax.random.fold_in(key, 31), DEVICES).astype(jnp.int32)
    offsets = jax.random.permutation(jax.random.fold_in(key, 32), DEVICES)[:P_DEV].astype(jnp.int32)
    senders = jnp.arange(DEVICES, dtype=jnp.int32)[:, None]
    owners = mapping[(senders + offsets[None, :]) % DEVICES]
    hottest = jax.random.randint(jax.random.fold_in(key, 33), (), 0, DEVICES).astype(jnp.int32)
    sends_hot = jnp.any(owners == hottest, axis=1)
    priority = jax.random.permutation(jax.random.fold_in(key, 34), DEVICES).astype(jnp.int32)
    score = jnp.where(sends_hot, DEVICES + priority, priority)
    order = jnp.argsort(score, stable=True)
    ranking = jnp.zeros((DEVICES,), jnp.int32).at[order].set(jnp.arange(DEVICES, dtype=jnp.int32))
    extra = ranking < 3 * P_DEV
    owners = owners.at[:, 0].set(jnp.where(extra, hottest, owners[:, 0]))
    within = jax.random.randint(jax.random.fold_in(key, 35), (DEVICES, P_DEV), 0, CL_DEV)
    return (owners * CL_DEV + within).reshape(PASSAGES).astype(jnp.int32)


def block_levels(stream_key, shape, pieces, low, high):
    loudness, own = 1.0, jax.random.fold_in(stream_key, 6)
    for position, parts in pieces:
        draws = jnp.exp(jax.random.uniform(jax.random.fold_in(own, position), (parts,), jnp.float32, low / len(pieces), high / len(pieces)))
        loudness = loudness * jnp.repeat(draws, shape[position] // parts).reshape([-1 if axis == position else 1 for axis in range(len(shape))])
    return loudness


def bell_draw(key, shape, deviation, reach, cuts=(), kind=jnp.bfloat16):
    entries = deviation * jax.random.normal(key, shape, jnp.float32)
    if cuts:
        entries = entries * block_levels(key, shape, cuts, -0.22, 0.18)
    return jnp.clip(entries, -reach, reach).astype(kind)


def setup_inputs(seed: int = 0) -> dict:
    key_of = jax.random.split(jax.random.key(seed), 14)
    hidden_states = draw_hidden_states(jax.random.fold_in(key_of[13], 71), 0)
    lengths = draw_lengths(jax.random.fold_in(key_of[13], 71), 0)
    block_list = draw_block_list(jax.random.fold_in(key_of[13], 71), 0)
    cluster_ids = draw_cluster_ids(jax.random.fold_in(key_of[13], 71), 0)
    attn_weight = draw_attn_weight(jax.random.fold_in(key_of[13], 71), 0)
    out_weight = bell_draw(key_of[5], (D, D), D ** -0.5, 0.21875)
    up_weight = bell_draw(key_of[6], (D, FF), D ** -0.5, 0.21875)
    down_weight = bell_draw(key_of[7], (FF, D), FF ** -0.5, 0.109375)
    head_weight = bell_draw(key_of[8], (D, D), D ** -0.5, 0.21875)
    head_gain = jnp.clip(1.0 + 0.18 * jax.random.normal(key_of[9], (D,), jnp.float32), 0.1, 1.9)
    vocab_weight = bell_draw(key_of[10], (VOCAB, D), D ** -0.5, 0.21875, ((0, 8),))
    vocab_bias = jnp.clip(2.0 * jax.random.uniform(key_of[11], (VOCAB,), jnp.float32) ** block_levels(key_of[11], (VOCAB,), ((0, 8),), -0.2, 0.2), 0.0, 2.0).astype(jnp.bfloat16)
    centroids = bell_draw(key_of[12], (CLUSTERS, D), 1.0, 6.0, ((0, 32),))
    return dict(hidden_states=hidden_states, lengths=lengths, block_list=block_list, cluster_ids=cluster_ids, attn_weight=attn_weight, out_weight=out_weight, up_weight=up_weight, down_weight=down_weight, head_weight=head_weight, head_gain=head_gain, vocab_weight=vocab_weight, vocab_bias=vocab_bias, centroids=centroids)


def layer_norm(values):
    center = values - lax.optimization_barrier(jnp.mean(values, axis=-1, keepdims=True))
    spread = lax.optimization_barrier(jnp.mean(center * center, axis=-1, keepdims=True))
    return center * lax.rsqrt(spread + 1e-06)

def encode(hidden_states, lengths, attn_weight, out_weight, up_weight, down_weight):
    passages = lengths.shape[0]
    seq_len = hidden_states.shape[0] // passages
    width = hidden_states.shape[1]
    head_count = width // HEAD
    joined = jnp.dot(hidden_states, attn_weight, preferred_element_type=jnp.float32).astype(jnp.bfloat16)
    joined = joined.reshape(passages, seq_len, 3, head_count, HEAD).astype(jnp.float32)
    query_heads = joined[:, :, 0]
    key_heads = joined[:, :, 1]
    value_heads = joined[:, :, 2]
    scores = jnp.einsum('pqhd,pkhd->phqk', query_heads, key_heads) / math.sqrt(HEAD)
    live_mask = jnp.arange(seq_len, dtype=jnp.int32)[None, :] < lengths[:, None]
    scores = jnp.where(live_mask[:, None, None, :], scores, -1e+30)
    highest = lax.optimization_barrier(jnp.max(scores, axis=-1, keepdims=True))
    expo = jnp.exp(scores - highest)
    attention = (expo / lax.optimization_barrier(jnp.sum(expo, axis=-1, keepdims=True))).astype(jnp.bfloat16)
    context = jnp.einsum('phqk,pkhd->pqhd', attention.astype(jnp.float32), value_heads)
    context = context.astype(jnp.bfloat16).reshape(passages * seq_len, width)
    mixed = hidden_states.astype(jnp.float32) + jnp.dot(context, out_weight, preferred_element_type=jnp.float32)
    first = layer_norm(mixed).astype(jnp.bfloat16)
    inner = jax.nn.gelu(jnp.dot(first, up_weight, preferred_element_type=jnp.float32), approximate=False).astype(jnp.bfloat16)
    second = first.astype(jnp.float32) + jnp.dot(inner, down_weight, preferred_element_type=jnp.float32)
    return layer_norm(second).astype(jnp.bfloat16)

def head_transform(layer_out, head_weight, head_gain):
    middle = jax.nn.gelu(jnp.dot(layer_out, head_weight, preferred_element_type=jnp.float32), approximate=False)
    return (layer_norm(middle) * head_gain[None, :]).astype(jnp.bfloat16)

def vocab_pool(transformed, lengths, block_list, vocab_weight, vocab_bias, first_col):
    logits = lax.dot_general(transformed, vocab_weight, (((1,), (1,)), ((), ())), preferred_element_type=jnp.float32)
    logits = logits + vocab_bias.astype(jnp.float32)[None, :]
    activity = jnp.log1p(jax.nn.relu(logits))
    passages = lengths.shape[0]
    seq_len = transformed.shape[0] // passages
    columns = vocab_weight.shape[0]
    activity = activity.reshape(passages, seq_len, columns)
    live_mask = (jnp.arange(seq_len, dtype=jnp.int32)[None, :] < lengths[:, None]).astype(jnp.float32)
    pooled = lax.optimization_barrier(jnp.max(activity * live_mask[:, :, None], axis=1))
    block_ids = (first_col + jnp.arange(columns, dtype=jnp.int32)) // BLOCK
    listed = jnp.any(block_list[:, :, None] == block_ids[None, None, :], axis=1)
    return jnp.where(listed, pooled, 0.0).astype(jnp.bfloat16)

def reference(hidden_states, lengths, block_list, cluster_ids, attn_weight, out_weight, up_weight, down_weight, head_weight, head_gain, vocab_weight, vocab_bias, centroids):

    def one_passage(inputs):
        tokens, length_one, listed_one = inputs
        layer_out = encode(tokens, length_one[None], attn_weight, out_weight, up_weight, down_weight)
        transformed = head_transform(layer_out, head_weight, head_gain)
        sparse_row = vocab_pool(transformed, length_one[None], listed_one[None, :], vocab_weight, vocab_bias, jnp.int32(0))
        return (sparse_row[0], layer_out[0])
    sparse_weights, dense_rows = lax.map(one_passage, (hidden_states.reshape(PASSAGES, SEQ, D), lengths, block_list))
    owner_ids = (cluster_ids // CL_DEV).astype(jnp.int32)
    residual = (dense_rows.astype(jnp.float32) - centroids[cluster_ids].astype(jnp.float32)).astype(jnp.bfloat16)
    places = jnp.arange(PASSAGES, dtype=jnp.int32)
    same_owner = owner_ids[:, None] == owner_ids[None, :]
    earlier = places[None, :] < places[:, None]
    ranks = lax.optimization_barrier(jnp.sum((same_owner & earlier).astype(jnp.int32), axis=1)).astype(jnp.int32)
    slot_index = (owner_ids * CAP + ranks).astype(jnp.int32)
    dense_flat = jnp.zeros((DEVICES * CAP, D), jnp.bfloat16).at[slot_index].set(residual)
    passage_flat = jnp.full((DEVICES * CAP,), -1, jnp.int32).at[slot_index].set(places)
    return (sparse_weights, dense_flat.reshape(DEVICES, CAP, D), passage_flat.reshape(DEVICES, CAP))
```

```python
import functools
import math

import jax
import jax.numpy as jnp
from jax import lax
from jax.experimental import pallas as pl
from jax.experimental.pallas import tpu as pltpu
from jax.sharding import PartitionSpec as P

HEAD = 64
BLOCK = 128
CL_DEV = 512
CAP = 16
MESH = pl.DeviceIdType.MESH
F32 = jnp.float32
BF16 = jnp.bfloat16


def norm(values):
    center = values - jnp.mean(values, axis=-1, keepdims=True)
    spread = jnp.mean(center * center, axis=-1, keepdims=True)
    return center * lax.rsqrt(spread + 1e-06)


def gelu(v):
    return (0.5 * v) * (1.0 + lax.erf(v * math.sqrt(0.5)))


def mm(a, b):
    return jnp.dot(a, b, preferred_element_type=F32)


def mm_nt(a, b):
    return lax.dot_general(a, b, (((1,), (1,)), ((), ())), preferred_element_type=F32)


def mm_tn(a, b):
    return lax.dot_general(a, b, (((0,), (0,)), ((), ())), preferred_element_type=F32)


def kernel(
    groups,
    n,
    side,
    seq,
    chunk_passages,
    hid_hbm,
    len_hbm,
    blk_hbm,
    cid_hbm,
    aw_hbm,
    ow_hbm,
    uw_hbm,
    dw_hbm,
    hw_hbm,
    gain_hbm,
    voc_hbm,
    bias_hbm,
    cen_hbm,
    sparse_out,
    dense_out,
    slot_out,
    hid,
    len_ref,
    blk,
    cid_ref,
    aw,
    ow,
    uw,
    dw,
    hw,
    gain,
    voc,
    bias,
    cen,
    gath,
    joined,
    ctx,
    fst,
    inner,
    dacc,
    payload,
    dall,
    res,
    wsem,
    tok_send,
    tok_recv,
    f_send,
    f_recv,
    d_send,
    d_recv,
    z_send,
    z_recv,
    x_send,
    x_recv,
):
    grp = lax.axis_index("grp")
    term = lax.axis_index("term")
    devices = groups * n
    me = grp * n + term
    chips = n // 2
    chip = term // 2
    core = term % 2
    partner = {"grp": grp, "term": chip * 2 + (1 - core)}
    cy, cx = chip // side, chip % side
    width = hid.shape[1]
    rows = chunk_passages * seq
    chunks = hid.shape[0] // rows
    ff = uw.shape[1]
    relay = side == 2
    half = seq // 2
    passages = len_ref.shape[0]
    split = width // 2
    tile = ff // 2

    def other(k):
        ky, kx = k // side, k % side
        to = ((cy + ky) % side) * side + (cx + kx) % side
        return {"grp": grp, "term": to * 2 + core}

    def source(k):
        ky, kx = k // side, k % side
        return ((cy + side - ky) % side) * side + (cx + side - kx) % side

    def everyone(d):
        to = (me + d) % devices
        return {"grp": to // n, "term": to % n}

    def load(i, src, dst):
        return pltpu.make_async_copy(src, dst, wsem.at[i])

    def hid_load(h):
        span = pl.ds(pl.multiple_of(h * rows, rows), rows)
        return load(h, hid_hbm.at[span], hid.at[span])

    def aw_load(c):
        cols = pl.ds(c * width, width)
        return load(chunks + c, aw_hbm.at[:, cols], aw.at[:, cols])

    def uw_load(j):
        cols = pl.ds(pl.multiple_of(j * tile, tile), tile)
        return load(chunks + 3 + j, uw_hbm.at[:, cols], uw.at[:, cols])

    base = chunks + 5
    ow_load = load(base, ow_hbm, ow)
    dw_load = load(base + 1, dw_hbm, dw)
    hw_load = load(base + 2, hw_hbm, hw)
    voc_load = load(base + 3, voc_hbm, voc)
    cen_load = load(base + 4, cen_hbm, cen)
    gain_load = load(base + 5, gain_hbm, gain)
    bias_load = load(base + 6, bias_hbm, bias)
    blk_load = load(base + 7, blk_hbm, blk)
    len_load = load(base + 8, len_hbm, len_ref)
    cid_load = load(base + 9, cid_hbm, cid_ref)

    hid_load(0).start()
    for c in range(3):
        aw_load(c).start()
    len_load.start()
    blk_load.start()
    cid_load.start()
    ow_load.start()

    barrier = pltpu.get_barrier_semaphore()

    @pl.loop(1, devices)
    def _(d):
        pl.semaphore_signal(barrier, inc=1, device_id=everyone(d), device_id_type=MESH)

    def seat(p):
        return pl.ds(pl.multiple_of(p * seq, seq), seq)

    def tok_copy(p, k):
        return pltpu.make_async_remote_copy(
            src_ref=gath.at[0, 0, seat(p)],
            dst_ref=gath.at[k, 0, seat(p)],
            send_sem=tok_send.at[p, k],
            recv_sem=tok_recv.at[p, k],
            device_id=other(k),
            device_id_type=MESH,
        )

    def relay_copy(p, part):
        via = 1 + part
        span = pl.ds(pl.multiple_of(p * seq + part * half, half), half)
        return pltpu.make_async_remote_copy(
            src_ref=gath.at[via, 0, span],
            dst_ref=gath.at[3, 0, span],
            send_sem=tok_send.at[p, 3 + part],
            recv_sem=tok_recv.at[p, 3 + part],
            device_id=other(2 - part),
            device_id_type=MESH,
        )

    def forward(p, k):
        return pltpu.make_async_remote_copy(
            src_ref=gath.at[k, 0, seat(p)],
            dst_ref=gath.at[k, 1, seat(p)],
            send_sem=f_send.at[p, k],
            recv_sem=f_recv.at[p, k],
            device_id=partner,
            device_id_type=MESH,
        )

    def plane_copy(k):
        return pltpu.make_async_remote_copy(
            src_ref=payload,
            dst_ref=dall.at[0, grp, chip],
            send_sem=d_send.at[k],
            recv_sem=d_recv.at[k],
            device_id=other(k),
            device_id_type=MESH,
        )

    def group_copy(j):
        return pltpu.make_async_remote_copy(
            src_ref=dall.at[0, grp],
            dst_ref=dall.at[0, grp],
            send_sem=z_send.at[j],
            recv_sem=z_recv.at[j],
            device_id={"grp": (grp + j) % groups, "term": term},
            device_id_type=MESH,
        )

    dense_forward = pltpu.make_async_remote_copy(
        src_ref=dall.at[0],
        dst_ref=dall.at[1],
        send_sem=x_send.at[0],
        recv_sem=x_recv.at[0],
        device_id=partner,
        device_id_type=MESH,
    )

    def send_direct(p):
        if relay:
            tok_copy(p, 1).start()
            tok_copy(p, 2).start()
        else:

            @pl.loop(1, chips)
            def _(k):
                tok_copy(p, k).start()

    def when_first(h, *waits):
        @pl.when(h == 0)
        def _():
            for copy in waits:
                copy.wait()

    listing = blk.shape[1]
    terms = voc_hbm.shape[0]
    blocks = n * terms // BLOCK
    blk_load.wait()
    cid_load.wait()
    dacc[:, split:] = jnp.zeros_like(dacc[:, split:])
    square = lax.broadcasted_iota(jnp.int32, (listing, listing), 0) == lax.broadcasted_iota(
        jnp.int32, (listing, listing), 1
    )
    block_lane = lax.broadcasted_iota(jnp.int32, (listing, blocks), 1).astype(F32)
    id_lane = lax.broadcasted_iota(jnp.int32, (1, 128), 1)
    for p in range(passages):
        line = blk[p : p + 1, :].astype(F32)
        column = jnp.sum(jnp.where(square, line, 0.0), axis=1, keepdims=True)
        marks = jnp.max(jnp.where(column == block_lane, 1.0, 0.0), axis=0, keepdims=True)
        dacc[p : p + 1, split : split + blocks] = marks
        cid = cid_ref[p]
        ids = jnp.where(id_lane == 0, cid // 256, jnp.where(id_lane == 1, cid % 256, 0))
        dacc[passages + p : passages + p + 1, split : split + 128] = ids.astype(F32)
    pairs = width // (2 * HEAD)
    low = lax.broadcasted_iota(jnp.int32, (seq, 2 * HEAD), 1) < HEAD
    key_place = lax.broadcasted_iota(jnp.int32, (seq, 2 * seq), 0)
    row_place = lax.broadcasted_iota(jnp.int32, (seq, width), 0)

    def encode(h, carry):
        hid_load(h).wait()
        when_first(h, aw_load(0))

        @pl.when(h == 0)
        def _():
            for j in range(2):
                uw_load(j).start()
            dw_load.start()
            hw_load.start()
            gain_load.start()

        x = hid[pl.ds(pl.multiple_of(h * rows, rows), rows), :]
        for c in range(3):
            if c > 0:
                when_first(h, aw_load(c))
            cols = slice(c * width, (c + 1) * width)
            joined[:, cols] = mm(x, aw[:, cols]).astype(BF16)

        @pl.when(h == 0)
        def _():
            len_load.wait()
            for i in range(1, chunks):
                hid_load(i).start()
            voc_load.start()
            bias_load.start()
            cen_load.start()

        def attend(p, carry):
            span = pl.ds(pl.multiple_of(p * seq, seq), seq)
            live = key_place < len_ref[h * chunk_passages + p]
            for pair in range(pairs):
                at = pair * 2 * HEAD
                q = joined[span, at : at + 2 * HEAD]
                k = joined[span, width + at : width + at + 2 * HEAD]
                v = joined[span, 2 * width + at : 2 * width + at + 2 * HEAD]
                zero = jnp.zeros_like(q)
                both = jnp.concatenate([jnp.where(low, q, zero), jnp.where(low, zero, q)], axis=0)
                scores = jnp.where(live, mm_nt(k, both), -1e30)
                top = jnp.max(scores, axis=0, keepdims=True)
                expo = jnp.exp2((scores - top) * (math.log2(math.e) / math.sqrt(HEAD)))
                att = (expo * (1.0 / jnp.sum(expo, axis=0, keepdims=True))).astype(BF16)
                mixed = mm_tn(att, v)
                ctx[span, at : at + 2 * HEAD] = jnp.where(low, mixed[:seq], mixed[seq:]).astype(BF16)
            return carry

        lax.fori_loop(0, chunk_passages, attend, 0)
        when_first(h, ow_load)
        fst[...] = norm(x.astype(F32) + mm(ctx[...], ow[...])).astype(BF16)

        def up(j, carry):
            when_first(h, uw_load(j))
            cols = pl.ds(pl.multiple_of(j * tile, tile), tile)
            inner[:, cols] = gelu(mm(fst[...], uw[:, cols])).astype(BF16)
            return carry

        lax.fori_loop(0, 2, up, 0)
        when_first(h, dw_load)
        layer_out = norm(fst[...].astype(F32) + mm(inner[...], dw[...])).astype(BF16)
        wide = layer_out.astype(F32)
        for i in range(chunk_passages):
            p = h * chunk_passages + i
            dacc[pl.ds(p, 1), 0:split] = wide[i * seq : i * seq + 1, :split]
            dacc[pl.ds(passages + p, 1), 0:split] = wide[i * seq : i * seq + 1, split:]

        @pl.when(h == 0)
        def _():
            pl.semaphore_wait(barrier, devices - 1)

        @pl.when(h == chunks - 1)
        def _():
            payload[...] = dacc[...].astype(BF16)
            dall[0, grp, chip] = payload[...]

            @pl.loop(1, chips)
            def _(k):
                plane_copy(k).start()

        when_first(h, hw_load, gain_load)
        out = norm(gelu(mm(layer_out, hw[...]))) * gain[...][None, :]

        for i in range(chunk_passages):
            p = h * chunk_passages + i
            one = out[i * seq : (i + 1) * seq]
            one = jnp.where(row_place < len_ref[p], one, one[0:1])
            gath[0, 0, seat(p), :] = one.astype(BF16)
        for i in range(chunk_passages):
            send_direct(h * chunk_passages + i)
        for i in range(chunk_passages):
            forward(h * chunk_passages + i, 0).start()
        return carry

    lax.fori_loop(0, chunks, encode, 0)

    wide_tile = min(2048, terms)

    def score(seats):
        spot = []
        for k, s, p in seats:
            c = source(k)
            cc = core if s == 0 else 1 - core
            spot.append((c * 2 + cc) * passages + p)

        for j in range(terms // wide_tile):
            cols = slice(j * wide_tile, (j + 1) * wide_tile)
            lhs = jnp.concatenate([gath[k, s, seat(p), :] for k, s, p in seats], axis=0)
            logits = mm_nt(lhs, voc[cols, :])
            for i, at in enumerate(spot):
                res[pl.ds(at, 1), cols] = jnp.max(
                    logits[i * seq : (i + 1) * seq], axis=0, keepdims=True
                )

    def exchange_groups():
        @pl.loop(1, chips)
        def _(k):
            plane_copy(k).wait_recv()

        @pl.loop(1, groups)
        def _(j):
            group_copy(j).start()

    def exchange_cores():
        @pl.loop(1, groups)
        def _(j):
            group_copy(j).wait_recv()

        dense_forward.start()

    def place():
        dense_forward.wait_recv()
        cen_load.wait()
        span = 2 * passages
        total = devices * span
        flat = dall[...].astype(F32).reshape(total, dall.shape[-1])
        facts = flat[:, split : split + 128].astype(BF16)
        pick = lax.broadcasted_iota(jnp.int32, (8, 128), 0) == lax.broadcasted_iota(
            jnp.int32, (8, 128), 1
        )
        pieces = pltpu.roll(
            mm_nt(jnp.where(pick, 1.0, 0.0).astype(BF16), facts), total - passages, 1
        )
        clusters = pieces[0:1] * 256.0 + pieces[1:2]

        def numbered(shape, axis):
            place = lax.broadcasted_iota(jnp.int32, shape, axis)
            sender, within = place // span, place % span
            stream, spot = sender // (groups * chips), sender % (groups * chips)
            cc = jnp.where(stream == 0, core, 1 - core)
            return (spot * 2 + cc) * passages + within, within

        passage, within = numbered((1, total), 1)
        above, _ = numbered((total, 1), 0)
        first = (me * CL_DEV).astype(F32)
        local = clusters - first
        own = (within < passages) & (local >= 0.0) & (local < CL_DEV)
        own = jnp.where(own, 1.0, 0.0)
        before = above < passage
        ranks = mm(
            jnp.broadcast_to(own, (8, total)).astype(BF16), jnp.where(before, 1.0, 0.0).astype(BF16)
        )[0:1]
        slot = lax.broadcasted_iota(jnp.int32, (CAP, total), 0).astype(F32)
        chosen = jnp.where((slot == ranks) & (own > 0.5), 1.0, 0.0)
        filled = jnp.sum(chosen, axis=1, keepdims=True) > 0.5
        number = jnp.sum(chosen * (passage.astype(F32) + 1.0), axis=1, keepdims=True) - 1.0
        local = jnp.where(own > 0.5, local, 0.0)
        entry = jnp.sum(chosen * local, axis=1, keepdims=True)
        both = jnp.concatenate([chosen, pltpu.roll(chosen, passages, 1)], axis=0).astype(BF16)
        picked = mm(both, flat[:, :split].astype(BF16))
        entries = lax.broadcasted_iota(jnp.int32, (CAP, CL_DEV), 1).astype(F32)
        lookup = jnp.where((entries == entry) & filled, 1.0, 0.0).astype(BF16)
        for part in range(2):
            cols = slice(part * split, (part + 1) * split)
            dense_out[0, :, cols] = jnp.where(
                filled, picked[part * CAP : (part + 1) * CAP] - mm(lookup, cen[:, cols]), 0.0
            ).astype(BF16)
        eye = lax.broadcasted_iota(jnp.int32, (CAP, CAP), 0) == lax.broadcasted_iota(
            jnp.int32, (CAP, CAP), 1
        )
        slot_out[...] = jnp.sum(jnp.where(eye, number, 0.0), axis=0, keepdims=True).astype(
            jnp.int32
        )

    def arrive(p):
        for part in range(2):
            tok_copy(p, 1 + part).wait_recv()
            relay_copy(p, part).start()
        for part in range(2):
            forward(p, 1 + part).start()

    def arrive_far(p):
        for part in range(2):
            relay_copy(p, part).wait_recv()
        forward(p, 3).start()

    voc_load.wait()
    bias_load.wait()
    if relay:
        arrive(0)

        @pl.loop(0, passages // 2)
        def _(i):
            for q in range(2):
                forward(2 * i + q, 0).wait_recv()
            score([(0, s, 2 * i + q) for s in range(2) for q in range(2)])

        @pl.loop(0, passages)
        def _(p):
            @pl.when(p < passages - 1)
            def _():
                arrive(p + 1)

            @pl.when(p == 1)
            def _():
                exchange_groups()

            for k in (1, 2):
                forward(p, k).wait_recv()
            score([(k, s, p) for k in (1, 2) for s in range(2)])

        arrive_far(0)

        @pl.loop(0, passages)
        def _(p):
            @pl.when(p == 0)
            def _():
                exchange_cores()

            @pl.when(p == 1)
            def _():
                place()

            @pl.when(p < passages - 1)
            def _():
                arrive_far(p + 1)

            forward(p, 3).wait_recv()
            score([(3, s, p) for s in range(2)])
    else:
        exchange_groups()

        @pl.loop(1, chips)
        def _(k):
            @pl.loop(0, passages)
            def _(p):
                tok_copy(p, k).wait_recv()
                forward(p, k).start()

        exchange_cores()

        @pl.loop(0, chips)
        def _(k):
            @pl.loop(0, passages)
            def _(p):
                forward(p, k).wait_recv()
                score([(k, s, p) for s in range(2)])

        place()

    marks = []
    for c in range(chips):
        for s in (core, 1 - core):
            marks.append(dall[s, grp, c, :, split : split + blocks].astype(F32)[:passages])
    marks = jnp.concatenate(marks, axis=0).astype(BF16)
    lead = term * (terms // BLOCK)
    offset = (lax.broadcasted_iota(jnp.int32, (blocks, terms), 0) - lead) * BLOCK
    column = lax.broadcasted_iota(jnp.int32, (blocks, terms), 1)
    spread = jnp.where((column >= offset) & (column < offset + BLOCK), 1.0, 0.0).astype(BF16)
    keep = mm(marks, spread) > 0.5
    raw = res[...] + bias[...].astype(F32)[None, :]
    sparse_out[...] = jnp.where(keep, jnp.log1p(jnp.maximum(raw, 0.0)), 0.0).astype(BF16)

    @pl.loop(1, chips)
    def _(k):
        plane_copy(k).wait_send()

    @pl.loop(1, groups)
    def _(j):
        group_copy(j).wait_send()

    dense_forward.wait_send()

    @pl.loop(0, passages)
    def _(p):
        @pl.loop(0, chips)
        def _(k):
            forward(p, k).wait_send()

        if relay:
            for part in range(2):
                tok_copy(p, 1 + part).wait_send()
                relay_copy(p, part).wait_send()
        else:

            @pl.loop(1, chips)
            def _(k):
                tok_copy(p, k).wait_send()


def finish(a_ref, b_ref, c_ref, a_out, b_out, c_out):
    a_out[...] = a_ref[...]
    b_out[...] = b_ref[...]
    c_out[...] = c_ref[...]


def body(
    groups,
    n,
    hidden,
    lengths,
    block_list,
    cluster_ids,
    attn_weight,
    out_weight,
    up_weight,
    down_weight,
    head_weight,
    head_gain,
    vocab_weight,
    vocab_bias,
    centroids,
):
    passages = lengths.shape[0]
    tokens, width = hidden.shape
    seq = tokens // passages
    ff = up_weight.shape[1]
    terms = vocab_weight.shape[0]
    devices = groups * n
    chips = n // 2
    side = math.isqrt(chips)
    chunk_passages = 2
    chunks = passages // chunk_passages
    rows = chunk_passages * seq
    packed = width // 2 + max(n * terms // BLOCK, 128)
    vm = pl.BlockSpec(memory_space=pltpu.VMEM)
    hbm = pl.BlockSpec(memory_space=pl.ANY)
    dma = pltpu.SemaphoreType.DMA
    operands = (
        hidden,
        lengths,
        block_list,
        cluster_ids,
        attn_weight,
        out_weight,
        up_weight,
        down_weight,
        head_weight,
        head_gain,
        vocab_weight,
        vocab_bias,
        centroids,
    )
    local = [
        (pltpu.SMEM if x is lengths or x is cluster_ids else pltpu.VMEM)(x.shape, x.dtype)
        for x in operands
    ]
    found = pl.pallas_call(
        functools.partial(kernel, groups, n, side, seq, chunk_passages),
        out_shape=(
            jax.ShapeDtypeStruct((n * passages, terms), BF16),
            jax.ShapeDtypeStruct((1, CAP, width), BF16),
            jax.ShapeDtypeStruct((1, CAP), jnp.int32),
        ),
        in_specs=[hbm] * 13,
        out_specs=(vm, vm, vm),
        scratch_shapes=local
        + [
            pltpu.VMEM((chips, 2, tokens, width), BF16),
            pltpu.VMEM((rows, 3 * width), BF16),
            pltpu.VMEM((rows, width), BF16),
            pltpu.VMEM((rows, width), BF16),
            pltpu.VMEM((rows, ff), BF16),
            pltpu.VMEM((2 * passages, packed), F32),
            pltpu.VMEM((2 * passages, packed), BF16),
            pltpu.VMEM((2, groups, chips, 2 * passages, packed), BF16),
            pltpu.VMEM((n * passages, terms), F32),
            dma((chunks + 15,)),
            dma((passages, chips + 1)),
            dma((passages, chips + 1)),
            dma((passages, chips)),
            dma((passages, chips)),
            dma((chips,)),
            dma((chips,)),
            dma((groups,)),
            dma((groups,)),
            dma((1,)),
            dma((1,)),
        ],
        compiler_params=pltpu.CompilerParams(
            collective_id=0, has_side_effects=True, vmem_limit_bytes=60 * 1024 * 1024
        ),
    )(*operands)
    return pl.pallas_call(
        finish,
        out_shape=tuple(jax.ShapeDtypeStruct(f.shape, f.dtype) for f in found),
        in_specs=[vm] * 3,
        out_specs=(vm,) * 3,
    )(*found)


def solution(mesh):
    placed = (
        P(("grp", "term"), None),
        P(("grp", "term")),
        P(("grp", "term"), None),
        P(("grp", "term")),
        P(),
        P(),
        P(),
        P(),
        P(),
        P(),
        P("term", None),
        P("term"),
        P(("grp", "term"), None),
    )
    return jax.shard_map(
        functools.partial(body, mesh.shape["grp"], mesh.shape["term"]),
        mesh=mesh,
        in_specs=placed,
        out_specs=(P("grp", "term"), P(("grp", "term"), None, None), P(("grp", "term"), None)),
        check_vma=False,
    )
```

```python
import functools
import math

import jax
import jax.numpy as jnp
from jax import lax
from jax.experimental import pallas as pl
from jax.experimental.pallas import tpu as pltpu
from jax.sharding import PartitionSpec as P

HEAD = 64
BLOCK = 128
CL_DEV = 512
CAP = 16
MESH = pl.DeviceIdType.MESH
F32 = jnp.float32
BF16 = jnp.bfloat16


def norm(values):
    center = values - jnp.mean(values, axis=-1, keepdims=True)
    spread = jnp.mean(center * center, axis=-1, keepdims=True)
    return center * lax.rsqrt(spread + 1e-06)


def gelu(v):
    return (0.5 * v) * (1.0 + lax.erf(v * math.sqrt(0.5)))


def mm(a, b):
    return jnp.dot(a, b, preferred_element_type=F32)


def mm_nt(a, b):
    return lax.dot_general(a, b, (((1,), (1,)), ((), ())), preferred_element_type=F32)


def kernel(
    groups,
    n,
    side,
    seq,
    chunk_passages,
    hid_hbm,
    len_hbm,
    blk_hbm,
    cid_hbm,
    aw_hbm,
    ow_hbm,
    uw_hbm,
    dw_hbm,
    hw_hbm,
    gain_hbm,
    voc_hbm,
    bias_hbm,
    cen_hbm,
    sparse_out,
    dense_out,
    slot_out,
    hid,
    len_ref,
    blk,
    cid_ref,
    aw,
    ow,
    uw,
    dw,
    hw,
    gain,
    voc,
    bias,
    cen,
    gath,
    joined,
    ctx,
    fst,
    inner,
    dacc,
    payload,
    dall,
    res,
    mask,
    wsem,
    tok_send,
    tok_recv,
    f_send,
    f_recv,
    d_send,
    d_recv,
    z_send,
    z_recv,
    x_send,
    x_recv,
):
    grp = lax.axis_index("grp")
    term = lax.axis_index("term")
    devices = groups * n
    me = grp * n + term
    chips = n // 2
    chip = term // 2
    core = term % 2
    partner = {"grp": grp, "term": chip * 2 + (1 - core)}
    cy, cx = chip // side, chip % side
    width = hid.shape[1]
    rows = chunk_passages * seq
    passages = len_ref.shape[0]
    chunks = passages // chunk_passages
    ff = uw.shape[1]
    relay = side == 2
    cut = seq // 2
    split = width // 2
    tile = ff // 2

    def other(k):
        ky, kx = k // side, k % side
        to = ((cy + ky) % side) * side + (cx + kx) % side
        return {"grp": grp, "term": to * 2 + core}

    def source(k):
        ky, kx = k // side, k % side
        return ((cy + side - ky) % side) * side + (cx + side - kx) % side

    def everyone(d):
        to = (me + d) % devices
        return {"grp": to // n, "term": to % n}

    def load(i, src, dst):
        return pltpu.make_async_copy(src, dst, wsem.at[i])

    def hid_load(h):
        span = pl.ds(pl.multiple_of(h * rows, rows), rows)
        return load(h, hid_hbm.at[span], hid.at[span])

    def aw_load(c):
        cols = pl.ds(c * width, width)
        return load(chunks + c, aw_hbm.at[:, cols], aw.at[:, cols])

    def uw_load(j):
        cols = pl.ds(pl.multiple_of(j * tile, tile), tile)
        return load(chunks + 3 + j, uw_hbm.at[:, cols], uw.at[:, cols])

    base = chunks + 5
    ow_load = load(base, ow_hbm, ow)
    dw_load = load(base + 1, dw_hbm, dw)
    hw_load = load(base + 2, hw_hbm, hw)
    voc_load = load(base + 3, voc_hbm, voc)
    cen_load = load(base + 4, cen_hbm, cen)
    gain_load = load(base + 5, gain_hbm, gain)
    bias_load = load(base + 6, bias_hbm, bias)
    blk_load = load(base + 7, blk_hbm, blk)
    len_load = load(base + 8, len_hbm, len_ref)
    cid_load = load(base + 9, cid_hbm, cid_ref)

    len_load.start()
    hid_load(0).start()
    for c in range(3):
        aw_load(c).start()
    ow_load.start()

    barrier = pltpu.get_barrier_semaphore()

    @pl.loop(1, devices)
    def _(d):
        pl.semaphore_signal(barrier, inc=1, device_id=everyone(d), device_id_type=MESH)

    def seat(p):
        return pl.ds(pl.multiple_of(p * seq, seq), seq)

    def tok_copy(p, k):
        return pltpu.make_async_remote_copy(
            src_ref=gath.at[0, 0, seat(p)],
            dst_ref=gath.at[k, 0, seat(p)],
            send_sem=tok_send.at[p, k],
            recv_sem=tok_recv.at[p, k],
            device_id=other(k),
            device_id_type=MESH,
        )

    def relay_copy(p, part):
        via = 1 + part
        start, size = ((0, cut), (cut, seq - cut))[part]
        span = pl.ds(pl.multiple_of(p * seq + start, 16), size)
        return pltpu.make_async_remote_copy(
            src_ref=gath.at[via, 0, span],
            dst_ref=gath.at[3, 0, span],
            send_sem=tok_send.at[p, 3 + part],
            recv_sem=tok_recv.at[p, 3 + part],
            device_id=other(2 - part),
            device_id_type=MESH,
        )

    def forward(p, k):
        return pltpu.make_async_remote_copy(
            src_ref=gath.at[k, 0, seat(p)],
            dst_ref=gath.at[k, 1, seat(p)],
            send_sem=f_send.at[p, k],
            recv_sem=f_recv.at[p, k],
            device_id=partner,
            device_id_type=MESH,
        )

    def plane_copy(k):
        return pltpu.make_async_remote_copy(
            src_ref=payload,
            dst_ref=dall.at[0, grp, chip],
            send_sem=d_send.at[k],
            recv_sem=d_recv.at[k],
            device_id=other(k),
            device_id_type=MESH,
        )

    def group_copy(j):
        return pltpu.make_async_remote_copy(
            src_ref=dall.at[0, grp],
            dst_ref=dall.at[0, grp],
            send_sem=z_send.at[j],
            recv_sem=z_recv.at[j],
            device_id={"grp": (grp + j) % groups, "term": term},
            device_id_type=MESH,
        )

    dense_forward = pltpu.make_async_remote_copy(
        src_ref=dall.at[0],
        dst_ref=dall.at[1],
        send_sem=x_send.at[0],
        recv_sem=x_recv.at[0],
        device_id=partner,
        device_id_type=MESH,
    )

    def send_direct(p):
        if relay:
            tok_copy(p, 1).start()
            tok_copy(p, 2).start()
        else:

            @pl.loop(1, chips)
            def _(k):
                tok_copy(p, k).start()

    listing = blk.shape[1]
    terms = voc_hbm.shape[0]
    blocks = n * terms // BLOCK
    pairs = width // (2 * HEAD)
    low = lax.broadcasted_iota(jnp.int32, (seq, 2 * HEAD), 1) < HEAD
    key_place = lax.broadcasted_iota(jnp.int32, (seq, 2 * seq), 0)
    upper = lax.broadcasted_iota(jnp.int32, (2 * HEAD, seq), 0) < HEAD
    row_place = lax.broadcasted_iota(jnp.int32, (seq, width), 0)

    def mark():
        blk_load.wait()
        cid_load.wait()
        dacc[:, split:] = jnp.zeros_like(dacc[:, split:])
        square = lax.broadcasted_iota(jnp.int32, (listing, listing), 0) == lax.broadcasted_iota(
            jnp.int32, (listing, listing), 1
        )
        block_lane = lax.broadcasted_iota(jnp.int32, (listing, blocks), 1).astype(F32)
        id_lane = lax.broadcasted_iota(jnp.int32, (1, 128), 1)
        for p in range(passages):
            line = blk[p : p + 1, :].astype(F32)
            column = jnp.sum(jnp.where(square, line, 0.0), axis=1, keepdims=True)
            marks = jnp.max(jnp.where(column == block_lane, 1.0, 0.0), axis=0, keepdims=True)
            dacc[p : p + 1, split : split + blocks] = marks
            cid = cid_ref[p]
            ids = jnp.where(id_lane == 0, cid // 256, jnp.where(id_lane == 1, cid % 256, 0))
            dacc[passages + p : passages + p + 1, split : split + 128] = ids.astype(F32)

    def attend(i, live):
        span = slice(i * seq, (i + 1) * seq)
        for pair in range(pairs):
            at = pair * 2 * HEAD
            q = joined[span, at : at + 2 * HEAD]
            k = joined[span, width + at : width + at + 2 * HEAD]
            v = joined[span, 2 * width + at : 2 * width + at + 2 * HEAD]
            zero = jnp.zeros_like(q)
            both = jnp.concatenate([jnp.where(low, q, zero), jnp.where(low, zero, q)], axis=0)
            scores = jnp.where(live, mm_nt(k, both), -1e30)
            top = jnp.max(scores, axis=0, keepdims=True)
            expo = jnp.exp2((scores - top) * (math.log2(math.e) / math.sqrt(HEAD)))
            scale = 1.0 / jnp.sum(expo, axis=0, keepdims=True)
            mixed = mm(v.T, expo.astype(BF16)) * scale
            ctx[span, at : at + 2 * HEAD] = jnp.where(upper, mixed[:, :seq], mixed[:, seq:]).astype(BF16).T

    def arrive(p):
        for part in range(2):
            tok_copy(p, 1 + part).wait_recv()
            relay_copy(p, part).start()
        for part in range(2):
            forward(p, 1 + part).start()

    def arrive_far(p):
        for part in range(2):
            relay_copy(p, part).wait_recv()
        forward(p, 3).start()

    def encode(h):
        hid_load(h).wait()
        if h == 0:
            aw_load(0).wait()
            for j in range(2):
                uw_load(j).start()
            dw_load.start()
            hw_load.start()
            gain_load.start()
        x = hid[h * rows : (h + 1) * rows, :]
        for c in range(3):
            if h == 0 and c > 0:
                aw_load(c).wait()
            cols = slice(c * width, (c + 1) * width)
            joined[:, cols] = mm(x, aw[:, cols]).astype(BF16)
        if h == 0:
            len_load.wait()
            for i in range(1, chunks):
                hid_load(i).start()
            voc_load.start()
            bias_load.start()
            blk_load.start()
            cid_load.start()
            cen_load.start()
        limits = [len_ref[h * chunk_passages + i] for i in range(chunk_passages)]
        for i in range(chunk_passages):
            attend(i, key_place < limits[i])
        if h == 0:
            ow_load.wait()
        fst[...] = norm(x.astype(F32) + mm(ctx[...], ow[...])).astype(BF16)
        if h == 0:
            for j in range(2):
                uw_load(j).wait()
        inner[...] = gelu(mm(fst[...], uw[...])).astype(BF16)
        if h == 0:
            dw_load.wait()
        layer_out = norm(fst[...].astype(F32) + mm(inner[...], dw[...])).astype(BF16)
        wide = layer_out.astype(F32)
        for i in range(chunk_passages):
            p = h * chunk_passages + i
            dacc[p : p + 1, 0:split] = wide[i * seq : i * seq + 1, :split]
            dacc[passages + p : passages + p + 1, 0:split] = wide[i * seq : i * seq + 1, split:]
        if h == 0:
            pl.semaphore_wait(barrier, devices - 1)
        if h == chunks - 1:
            mark()
            payload[...] = dacc[...].astype(BF16)
            dall[0, grp, chip] = payload[...]

            @pl.loop(1, chips)
            def _(k):
                plane_copy(k).start()

        if h == 0:
            hw_load.wait()
            gain_load.wait()
        out = norm(gelu(mm(layer_out, hw[...]))) * gain[...][None, :]
        for i in range(chunk_passages):
            p = h * chunk_passages + i
            one = out[i * seq : (i + 1) * seq]
            one = jnp.where(row_place < limits[i], one, one[0:1])
            gath[0, 0, p * seq : (p + 1) * seq, :] = one.astype(BF16)
            send_direct(p)
        for i in range(chunk_passages):
            forward(h * chunk_passages + i, 0).start()

    for h in range(chunks):
        encode(h)

    wide_tile = min(2048, terms)

    def score(seats):
        spot = []
        for k, s, p in seats:
            c = source(k)
            cc = core if s == 0 else 1 - core
            spot.append((c * 2 + cc) * passages + p)

        for j in range(terms // wide_tile):
            cols = slice(j * wide_tile, (j + 1) * wide_tile)
            lhs = jnp.concatenate([gath[k, s, seat(p), :] for k, s, p in seats], axis=0)
            logits = mm_nt(lhs, voc[cols, :])
            for i, at in enumerate(spot):
                res[pl.ds(at, 1), cols] = jnp.max(
                    logits[i * seq : (i + 1) * seq], axis=0, keepdims=True
                )

    def exchange_groups():
        @pl.loop(1, chips)
        def _(k):
            plane_copy(k).wait_recv()

        @pl.loop(1, groups)
        def _(j):
            group_copy(j).start()

    def exchange_cores():
        @pl.loop(1, groups)
        def _(j):
            group_copy(j).wait_recv()

        dense_forward.start()

    def place():
        dense_forward.wait_recv()
        cen_load.wait()
        span = 2 * passages
        total = devices * span
        flat = dall[...].astype(F32).reshape(total, dall.shape[-1])
        facts = flat[:, split : split + 128].astype(BF16)
        pick = lax.broadcasted_iota(jnp.int32, (8, 128), 0) == lax.broadcasted_iota(
            jnp.int32, (8, 128), 1
        )
        pieces = pltpu.roll(
            mm_nt(jnp.where(pick, 1.0, 0.0).astype(BF16), facts), total - passages, 1
        )
        clusters = pieces[0:1] * 256.0 + pieces[1:2]

        def numbered(shape, axis):
            place = lax.broadcasted_iota(jnp.int32, shape, axis)
            sender, within = place // span, place % span
            stream, spot = sender // (groups * chips), sender % (groups * chips)
            cc = jnp.where(stream == 0, core, 1 - core)
            return (spot * 2 + cc) * passages + within, within

        passage, within = numbered((1, total), 1)
        above, _ = numbered((total, 1), 0)
        first = (me * CL_DEV).astype(F32)
        local = clusters - first
        own = (within < passages) & (local >= 0.0) & (local < CL_DEV)
        own = jnp.where(own, 1.0, 0.0)
        before = above < passage
        ranks = mm(
            jnp.broadcast_to(own, (8, total)).astype(BF16), jnp.where(before, 1.0, 0.0).astype(BF16)
        )[0:1]
        slot = lax.broadcasted_iota(jnp.int32, (CAP, total), 0).astype(F32)
        chosen = jnp.where((slot == ranks) & (own > 0.5), 1.0, 0.0)
        filled = jnp.sum(chosen, axis=1, keepdims=True) > 0.5
        number = jnp.sum(chosen * (passage.astype(F32) + 1.0), axis=1, keepdims=True) - 1.0
        local = jnp.where(own > 0.5, local, 0.0)
        entry = jnp.sum(chosen * local, axis=1, keepdims=True)
        both = jnp.concatenate([chosen, pltpu.roll(chosen, passages, 1)], axis=0).astype(BF16)
        picked = mm(both, flat[:, :split].astype(BF16))
        entries = lax.broadcasted_iota(jnp.int32, (CAP, CL_DEV), 1).astype(F32)
        lookup = jnp.where((entries == entry) & filled, 1.0, 0.0).astype(BF16)
        for part in range(2):
            cols = slice(part * split, (part + 1) * split)
            dense_out[0, :, cols] = jnp.where(
                filled, picked[part * CAP : (part + 1) * CAP] - mm(lookup, cen[:, cols]), 0.0
            ).astype(BF16)
        eye = lax.broadcasted_iota(jnp.int32, (CAP, CAP), 0) == lax.broadcasted_iota(
            jnp.int32, (CAP, CAP), 1
        )
        slot_out[...] = jnp.sum(jnp.where(eye, number, 0.0), axis=0, keepdims=True).astype(
            jnp.int32
        )
        marks = []
        for c in range(chips):
            for s in (core, 1 - core):
                marks.append(dall[s, grp, c, :, split : split + blocks].astype(F32)[:passages])
        marks = jnp.concatenate(marks, axis=0).astype(BF16)
        lead = term * (terms // BLOCK)
        offset = (lax.broadcasted_iota(jnp.int32, (blocks, terms), 0) - lead) * BLOCK
        column = lax.broadcasted_iota(jnp.int32, (blocks, terms), 1)
        spread = jnp.where((column >= offset) & (column < offset + BLOCK), 1.0, 0.0).astype(BF16)
        mask[...] = mm(marks, spread)

    def settle():
        @pl.loop(1, chips)
        def _(k):
            plane_copy(k).wait_send()

        @pl.loop(1, groups)
        def _(j):
            group_copy(j).wait_send()

        dense_forward.wait_send()

        @pl.loop(0, passages)
        def _(p):
            @pl.loop(0, chips - 1 if relay else chips)
            def _(k):
                forward(p, k).wait_send()

            if relay:
                for part in range(2):
                    tok_copy(p, 1 + part).wait_send()
                    relay_copy(p, part).wait_send()
            else:

                @pl.loop(1, chips)
                def _(k):
                    tok_copy(p, k).wait_send()

        if relay:

            @pl.loop(0, passages - 1)
            def _(p):
                forward(p, 3).wait_send()

    voc_load.wait()
    bias_load.wait()
    if relay:
        last = passages - 1
        arrive(0)

        @pl.loop(0, passages // 2)
        def _(i):
            for q in range(2):
                forward(2 * i + q, 0).wait_recv()
            score([(0, s, 2 * i + q) for s in range(2) for q in range(2)])

        @pl.loop(0, passages)
        def _(p):
            @pl.when(p < last)
            def _():
                arrive(p + 1)

            @pl.when(p == 1)
            def _():
                exchange_groups()

            for k in (1, 2):
                forward(p, k).wait_recv()
            score([(k, s, p) for k in (1, 2) for s in range(2)])

        arrive_far(0)

        @pl.loop(0, passages)
        def _(p):
            @pl.when(p == 0)
            def _():
                exchange_cores()

            @pl.when(p == 1)
            def _():
                place()

            @pl.when(p < last)
            def _():
                arrive_far(p + 1)

            @pl.when(p == last)
            def _():
                settle()

            forward(p, 3).wait_recv()
            score([(3, s, p) for s in range(2)])

        forward(last, 3).wait_send()
    else:
        exchange_groups()

        @pl.loop(1, chips)
        def _(k):
            @pl.loop(0, passages)
            def _(p):
                tok_copy(p, k).wait_recv()
                forward(p, k).start()

        exchange_cores()

        @pl.loop(0, chips)
        def _(k):
            @pl.loop(0, passages)
            def _(p):
                forward(p, k).wait_recv()
                score([(k, s, p) for s in range(2)])

        place()
        settle()

    raw = res[...] + bias[...].astype(F32)[None, :]
    sparse_out[...] = jnp.where(mask[...] > 0.5, jnp.log1p(jnp.maximum(raw, 0.0)), 0.0).astype(BF16)


def finish(a_ref, b_ref, c_ref, a_out, b_out, c_out):
    a_out[...] = a_ref[...]
    b_out[...] = b_ref[...]
    c_out[...] = c_ref[...]


def body(
    groups,
    n,
    hidden,
    lengths,
    block_list,
    cluster_ids,
    attn_weight,
    out_weight,
    up_weight,
    down_weight,
    head_weight,
    head_gain,
    vocab_weight,
    vocab_bias,
    centroids,
):
    passages = lengths.shape[0]
    tokens, width = hidden.shape
    seq = tokens // passages
    ff = up_weight.shape[1]
    terms = vocab_weight.shape[0]
    devices = groups * n
    chips = n // 2
    side = math.isqrt(chips)
    chunk_passages = 2
    chunks = passages // chunk_passages
    rows = chunk_passages * seq
    packed = width // 2 + max(n * terms // BLOCK, 128)
    vm = pl.BlockSpec(memory_space=pltpu.VMEM)
    hbm = pl.BlockSpec(memory_space=pl.ANY)
    dma = pltpu.SemaphoreType.DMA
    operands = (
        hidden,
        lengths,
        block_list,
        cluster_ids,
        attn_weight,
        out_weight,
        up_weight,
        down_weight,
        head_weight,
        head_gain,
        vocab_weight,
        vocab_bias,
        centroids,
    )
    local = [
        (pltpu.SMEM if x is lengths or x is cluster_ids else pltpu.VMEM)(x.shape, x.dtype)
        for x in operands
    ]
    found = pl.pallas_call(
        functools.partial(kernel, groups, n, side, seq, chunk_passages),
        out_shape=(
            jax.ShapeDtypeStruct((n * passages, terms), BF16),
            jax.ShapeDtypeStruct((1, CAP, width), BF16),
            jax.ShapeDtypeStruct((1, CAP), jnp.int32),
        ),
        in_specs=[hbm] * 13,
        out_specs=(vm, vm, vm),
        scratch_shapes=local
        + [
            pltpu.VMEM((chips, 2, tokens, width), BF16),
            pltpu.VMEM((rows, 3 * width), BF16),
            pltpu.VMEM((rows, width), BF16),
            pltpu.VMEM((rows, width), BF16),
            pltpu.VMEM((rows, ff), BF16),
            pltpu.VMEM((2 * passages, packed), F32),
            pltpu.VMEM((2 * passages, packed), BF16),
            pltpu.VMEM((2, groups, chips, 2 * passages, packed), BF16),
            pltpu.VMEM((n * passages, terms), F32),
            pltpu.VMEM((n * passages, terms), F32),
            dma((chunks + 15,)),
            dma((passages, chips + 1)),
            dma((passages, chips + 1)),
            dma((passages, chips)),
            dma((passages, chips)),
            dma((chips,)),
            dma((chips,)),
            dma((groups,)),
            dma((groups,)),
            dma((1,)),
            dma((1,)),
        ],
        compiler_params=pltpu.CompilerParams(
            collective_id=0, has_side_effects=True, vmem_limit_bytes=60 * 1024 * 1024
        ),
    )(*operands)
    return pl.pallas_call(
        finish,
        out_shape=tuple(jax.ShapeDtypeStruct(f.shape, f.dtype) for f in found),
        in_specs=[vm] * 3,
        out_specs=(vm,) * 3,
    )(*found)


def solution(mesh):
    placed = (
        P(("grp", "term"), None),
        P(("grp", "term")),
        P(("grp", "term"), None),
        P(("grp", "term")),
        P(),
        P(),
        P(),
        P(),
        P(),
        P(),
        P("term", None),
        P("term"),
        P(("grp", "term"), None),
    )
    return jax.shard_map(
        functools.partial(body, mesh.shape["grp"], mesh.shape["term"]),
        mesh=mesh,
        in_specs=placed,
        out_specs=(P("grp", "term"), P(("grp", "term"), None, None), P(("grp", "term"), None)),
        check_vma=False,
    )
```

```python
import functools
import math

import jax
import jax.numpy as jnp
from jax import lax
from jax.experimental import pallas as pl
from jax.experimental.pallas import tpu as pltpu
from jax.sharding import PartitionSpec as P

HEAD = 64
BLOCK = 128
CL_DEV = 512
CAP = 16
MESH = pl.DeviceIdType.MESH
F32 = jnp.float32
BF16 = jnp.bfloat16


def norm(values):
    center = values - jnp.mean(values, axis=-1, keepdims=True)
    spread = jnp.mean(center * center, axis=-1, keepdims=True)
    return center * lax.rsqrt(spread + 1e-06)


def gelu(v):
    return (0.5 * v) * (1.0 + lax.erf(v * math.sqrt(0.5)))


def mm(a, b):
    return jnp.dot(a, b, preferred_element_type=F32)


def mm_nt(a, b):
    return lax.dot_general(a, b, (((1,), (1,)), ((), ())), preferred_element_type=F32)


def kernel(
    groups,
    n,
    side,
    seq,
    chunk_passages,
    hid_hbm,
    len_hbm,
    blk_hbm,
    cid_hbm,
    aw_hbm,
    ow_hbm,
    uw_hbm,
    dw_hbm,
    hw_hbm,
    gain_hbm,
    voc_hbm,
    bias_hbm,
    cen_hbm,
    sparse_out,
    dense_out,
    slot_out,
    hid,
    len_ref,
    blk,
    cid_ref,
    aw,
    ow,
    uw,
    dw,
    hw,
    gain,
    voc,
    bias,
    cen,
    gath,
    joined,
    ctx,
    fst,
    inner,
    dacc,
    payload,
    dall,
    res,
    mask,
    wsem,
    tok_send,
    tok_recv,
    f_send,
    f_recv,
    d_send,
    d_recv,
    z_send,
    z_recv,
    x_send,
    x_recv,
):
    grp = lax.axis_index("grp")
    term = lax.axis_index("term")
    devices = groups * n
    me = grp * n + term
    chips = n // 2
    chip = term // 2
    core = term % 2
    partner = {"grp": grp, "term": chip * 2 + (1 - core)}
    cy, cx = chip // side, chip % side
    width = hid.shape[1]
    rows = chunk_passages * seq
    passages = len_ref.shape[0]
    chunks = passages // chunk_passages
    ff = uw.shape[1]
    relay = side == 2
    cut = seq // 2
    split = width // 2
    tile = ff // 2

    def other(k):
        ky, kx = k // side, k % side
        to = ((cy + ky) % side) * side + (cx + kx) % side
        return {"grp": grp, "term": to * 2 + core}

    def source(k):
        ky, kx = k // side, k % side
        return ((cy + side - ky) % side) * side + (cx + side - kx) % side

    def everyone(d):
        to = (me + d) % devices
        return {"grp": to // n, "term": to % n}

    def load(i, src, dst):
        return pltpu.make_async_copy(src, dst, wsem.at[i])

    def hid_load(h):
        span = pl.ds(pl.multiple_of(h * rows, rows), rows)
        return load(h, hid_hbm.at[span], hid.at[span])

    def aw_load(c):
        cols = pl.ds(c * width, width)
        return load(chunks + c, aw_hbm.at[:, cols], aw.at[:, cols])

    def uw_load(j):
        cols = pl.ds(pl.multiple_of(j * tile, tile), tile)
        return load(chunks + 3 + j, uw_hbm.at[:, cols], uw.at[:, cols])

    base = chunks + 5
    ow_load = load(base, ow_hbm, ow)
    dw_load = load(base + 1, dw_hbm, dw)
    hw_load = load(base + 2, hw_hbm, hw)
    voc_load = load(base + 3, voc_hbm, voc)
    cen_load = load(base + 4, cen_hbm, cen)
    gain_load = load(base + 5, gain_hbm, gain)
    bias_load = load(base + 6, bias_hbm, bias)
    blk_load = load(base + 7, blk_hbm, blk)
    len_load = load(base + 8, len_hbm, len_ref)
    cid_load = load(base + 9, cid_hbm, cid_ref)

    len_load.start()
    hid_load(0).start()
    for c in range(3):
        aw_load(c).start()
    ow_load.start()

    barrier = pltpu.get_barrier_semaphore()

    @pl.loop(1, devices)
    def _(d):
        pl.semaphore_signal(barrier, inc=1, device_id=everyone(d), device_id_type=MESH)

    def seat(p):
        return pl.ds(pl.multiple_of(p * seq, seq), seq)

    def tok_copy(p, k):
        return pltpu.make_async_remote_copy(
            src_ref=gath.at[0, 0, seat(p)],
            dst_ref=gath.at[k, 0, seat(p)],
            send_sem=tok_send.at[p, k],
            recv_sem=tok_recv.at[p, k],
            device_id=other(k),
            device_id_type=MESH,
        )

    def relay_copy(p, part):
        via = 1 + part
        start, size = ((0, cut), (cut, seq - cut))[part]
        span = pl.ds(pl.multiple_of(p * seq + start, 16), size)
        return pltpu.make_async_remote_copy(
            src_ref=gath.at[via, 0, span],
            dst_ref=gath.at[3, 0, span],
            send_sem=tok_send.at[p, 3 + part],
            recv_sem=tok_recv.at[p, 3 + part],
            device_id=other(2 - part),
            device_id_type=MESH,
        )

    def forward(p, k):
        return pltpu.make_async_remote_copy(
            src_ref=gath.at[k, 0, seat(p)],
            dst_ref=gath.at[k, 1, seat(p)],
            send_sem=f_send.at[p, k],
            recv_sem=f_recv.at[p, k],
            device_id=partner,
            device_id_type=MESH,
        )

    def plane_copy(k):
        return pltpu.make_async_remote_copy(
            src_ref=payload,
            dst_ref=dall.at[0, grp, chip],
            send_sem=d_send.at[k],
            recv_sem=d_recv.at[k],
            device_id=other(k),
            device_id_type=MESH,
        )

    def group_copy(j):
        return pltpu.make_async_remote_copy(
            src_ref=dall.at[0, grp],
            dst_ref=dall.at[0, grp],
            send_sem=z_send.at[j],
            recv_sem=z_recv.at[j],
            device_id={"grp": (grp + j) % groups, "term": term},
            device_id_type=MESH,
        )

    dense_forward = pltpu.make_async_remote_copy(
        src_ref=dall.at[0],
        dst_ref=dall.at[1],
        send_sem=x_send.at[0],
        recv_sem=x_recv.at[0],
        device_id=partner,
        device_id_type=MESH,
    )

    def send_direct(p):
        if relay:
            tok_copy(p, 1).start()
            tok_copy(p, 2).start()
        else:

            @pl.loop(1, chips)
            def _(k):
                tok_copy(p, k).start()

    listing = blk.shape[1]
    terms = voc_hbm.shape[0]
    blocks = n * terms // BLOCK
    pairs = width // (2 * HEAD)
    low = lax.broadcasted_iota(jnp.int32, (seq, 2 * HEAD), 1) < HEAD
    key_place = lax.broadcasted_iota(jnp.int32, (seq, 2 * seq), 0)
    upper = lax.broadcasted_iota(jnp.int32, (2 * HEAD, seq), 0) < HEAD
    row_place = lax.broadcasted_iota(jnp.int32, (seq, width), 0)

    def mark():
        blk_load.wait()
        cid_load.wait()
        dacc[:, split:] = jnp.zeros_like(dacc[:, split:])
        square = lax.broadcasted_iota(jnp.int32, (listing, listing), 0) == lax.broadcasted_iota(
            jnp.int32, (listing, listing), 1
        )
        block_lane = lax.broadcasted_iota(jnp.int32, (listing, blocks), 1).astype(F32)
        id_lane = lax.broadcasted_iota(jnp.int32, (1, 128), 1)
        for p in range(passages):
            line = blk[p : p + 1, :].astype(F32)
            column = jnp.sum(jnp.where(square, line, 0.0), axis=1, keepdims=True)
            marks = jnp.max(jnp.where(column == block_lane, 1.0, 0.0), axis=0, keepdims=True)
            dacc[p : p + 1, split : split + blocks] = marks
            cid = cid_ref[p]
            ids = jnp.where(id_lane == 0, cid // 256, jnp.where(id_lane == 1, cid % 256, 0))
            dacc[passages + p : passages + p + 1, split : split + 128] = ids.astype(F32)

    def attend(i, live):
        span = slice(i * seq, (i + 1) * seq)
        for pair in range(pairs):
            at = pair * 2 * HEAD
            q = joined[span, at : at + 2 * HEAD]
            k = joined[span, width + at : width + at + 2 * HEAD]
            v = joined[span, 2 * width + at : 2 * width + at + 2 * HEAD]
            zero = jnp.zeros_like(q)
            both = jnp.concatenate([jnp.where(low, q, zero), jnp.where(low, zero, q)], axis=0)
            scores = jnp.where(live, mm_nt(k, both), -1e30)
            top = jnp.max(scores, axis=0, keepdims=True)
            expo = jnp.exp2((scores - top) * (math.log2(math.e) / math.sqrt(HEAD)))
            scale = 1.0 / jnp.sum(expo, axis=0, keepdims=True)
            mixed = mm(v.T, expo.astype(BF16)) * scale
            ctx[span, at : at + 2 * HEAD] = jnp.where(upper, mixed[:, :seq], mixed[:, seq:]).astype(BF16).T

    def arrive(p):
        for part in range(2):
            tok_copy(p, 1 + part).wait_recv()
            relay_copy(p, part).start()
        for part in range(2):
            forward(p, 1 + part).start()

    def arrive_far(p):
        for part in range(2):
            relay_copy(p, part).wait_recv()
        forward(p, 3).start()

    def encode(h):
        hid_load(h).wait()
        if h == 0:
            aw_load(0).wait()
            for j in range(2):
                uw_load(j).start()
            dw_load.start()
            hw_load.start()
            gain_load.start()
        x = hid[h * rows : (h + 1) * rows, :]
        for c in range(3):
            if h == 0 and c > 0:
                aw_load(c).wait()
            cols = slice(c * width, (c + 1) * width)
            joined[:, cols] = mm(x, aw[:, cols]).astype(BF16)
        if h == 0:
            len_load.wait()
            for i in range(1, chunks):
                hid_load(i).start()
            voc_load.start()
            bias_load.start()
            blk_load.start()
            cid_load.start()
            cen_load.start()
        limits = [len_ref[h * chunk_passages + i] for i in range(chunk_passages)]
        for i in range(chunk_passages):
            attend(i, key_place < limits[i])
        if h == 0:
            ow_load.wait()
        fst[...] = norm(x.astype(F32) + mm(ctx[...], ow[...])).astype(BF16)
        if h == 0:
            for j in range(2):
                uw_load(j).wait()
        inner[...] = gelu(mm(fst[...], uw[...])).astype(BF16)
        if h == 0:
            dw_load.wait()
        layer_out = norm(fst[...].astype(F32) + mm(inner[...], dw[...])).astype(BF16)
        wide = layer_out.astype(F32)
        for i in range(chunk_passages):
            p = h * chunk_passages + i
            dacc[p : p + 1, 0:split] = wide[i * seq : i * seq + 1, :split]
            dacc[passages + p : passages + p + 1, 0:split] = wide[i * seq : i * seq + 1, split:]
        if h == 0:
            pl.semaphore_wait(barrier, devices - 1)
        if h == chunks - 1:
            mark()
            payload[...] = dacc[...].astype(BF16)
            dall[0, grp, chip] = payload[...]

            @pl.loop(1, chips)
            def _(k):
                plane_copy(k).start()

        if h == 0:
            hw_load.wait()
            gain_load.wait()
        out = norm(gelu(mm(layer_out, hw[...]))) * gain[...][None, :]
        for i in range(chunk_passages):
            p = h * chunk_passages + i
            one = out[i * seq : (i + 1) * seq]
            one = jnp.where(row_place < limits[i], one, one[0:1])
            gath[0, 0, p * seq : (p + 1) * seq, :] = one.astype(BF16)
            send_direct(p)
        for i in range(chunk_passages):
            forward(h * chunk_passages + i, 0).start()

    for h in range(chunks):
        encode(h)

    wide_tile = min(2048, terms)

    def score(seats):
        spot = []
        for k, s, p in seats:
            c = source(k)
            cc = core if s == 0 else 1 - core
            spot.append((c * 2 + cc) * passages + p)

        for j in range(terms // wide_tile):
            cols = slice(j * wide_tile, (j + 1) * wide_tile)
            lhs = jnp.concatenate([gath[k, s, seat(p), :] for k, s, p in seats], axis=0)
            logits = mm_nt(lhs, voc[cols, :])
            for i, at in enumerate(spot):
                res[pl.ds(at, 1), cols] = jnp.max(
                    logits[i * seq : (i + 1) * seq], axis=0, keepdims=True
                )

    def exchange_groups():
        @pl.loop(1, chips)
        def _(k):
            plane_copy(k).wait_recv()

        @pl.loop(1, groups)
        def _(j):
            group_copy(j).start()

    def exchange_cores():
        @pl.loop(1, groups)
        def _(j):
            group_copy(j).wait_recv()

        dense_forward.start()

    def place():
        dense_forward.wait_recv()
        cen_load.wait()
        span = 2 * passages
        total = devices * span
        flat = dall[...].astype(F32).reshape(total, dall.shape[-1])
        facts = flat[:, split : split + 128].astype(BF16)
        pick = lax.broadcasted_iota(jnp.int32, (8, 128), 0) == lax.broadcasted_iota(
            jnp.int32, (8, 128), 1
        )
        pieces = pltpu.roll(
            mm_nt(jnp.where(pick, 1.0, 0.0).astype(BF16), facts), total - passages, 1
        )
        clusters = pieces[0:1] * 256.0 + pieces[1:2]

        def numbered(shape, axis):
            place = lax.broadcasted_iota(jnp.int32, shape, axis)
            sender, within = place // span, place % span
            stream, spot = sender // (groups * chips), sender % (groups * chips)
            cc = jnp.where(stream == 0, core, 1 - core)
            return (spot * 2 + cc) * passages + within, within

        passage, within = numbered((1, total), 1)
        above, _ = numbered((total, 1), 0)
        first = (me * CL_DEV).astype(F32)
        local = clusters - first
        own = (within < passages) & (local >= 0.0) & (local < CL_DEV)
        own = jnp.where(own, 1.0, 0.0)
        before = above < passage
        ranks = mm(
            jnp.broadcast_to(own, (8, total)).astype(BF16), jnp.where(before, 1.0, 0.0).astype(BF16)
        )[0:1]
        slot = lax.broadcasted_iota(jnp.int32, (CAP, total), 0).astype(F32)
        chosen = jnp.where((slot == ranks) & (own > 0.5), 1.0, 0.0)
        filled = jnp.sum(chosen, axis=1, keepdims=True) > 0.5
        number = jnp.sum(chosen * (passage.astype(F32) + 1.0), axis=1, keepdims=True) - 1.0
        local = jnp.where(own > 0.5, local, 0.0)
        entry = jnp.sum(chosen * local, axis=1, keepdims=True)
        both = jnp.concatenate([chosen, pltpu.roll(chosen, passages, 1)], axis=0).astype(BF16)
        picked = mm(both, flat[:, :split].astype(BF16))
        entries = lax.broadcasted_iota(jnp.int32, (CAP, CL_DEV), 1).astype(F32)
        lookup = jnp.where((entries == entry) & filled, 1.0, 0.0).astype(BF16)
        for part in range(2):
            cols = slice(part * split, (part + 1) * split)
            dense_out[0, :, cols] = jnp.where(
                filled, picked[part * CAP : (part + 1) * CAP] - mm(lookup, cen[:, cols]), 0.0
            ).astype(BF16)
        eye = lax.broadcasted_iota(jnp.int32, (CAP, CAP), 0) == lax.broadcasted_iota(
            jnp.int32, (CAP, CAP), 1
        )
        slot_out[...] = jnp.sum(jnp.where(eye, number, 0.0), axis=0, keepdims=True).astype(
            jnp.int32
        )
        marks = []
        for c in range(chips):
            for s in (core, 1 - core):
                marks.append(dall[s, grp, c, :, split : split + blocks].astype(F32)[:passages])
        marks = jnp.concatenate(marks, axis=0).astype(BF16)
        lead = term * (terms // BLOCK)
        offset = (lax.broadcasted_iota(jnp.int32, (blocks, terms), 0) - lead) * BLOCK
        column = lax.broadcasted_iota(jnp.int32, (blocks, terms), 1)
        spread = jnp.where((column >= offset) & (column < offset + BLOCK), 1.0, 0.0).astype(BF16)
        mask[...] = mm(marks, spread)

    def settle():
        @pl.loop(1, chips)
        def _(k):
            plane_copy(k).wait_send()

        @pl.loop(1, groups)
        def _(j):
            group_copy(j).wait_send()

        dense_forward.wait_send()

        @pl.loop(0, passages)
        def _(p):
            @pl.loop(0, chips - 1 if relay else chips)
            def _(k):
                forward(p, k).wait_send()

            if relay:
                for part in range(2):
                    tok_copy(p, 1 + part).wait_send()
                    relay_copy(p, part).wait_send()
            else:

                @pl.loop(1, chips)
                def _(k):
                    tok_copy(p, k).wait_send()

        if relay:

            @pl.loop(0, passages - 1)
            def _(p):
                forward(p, 3).wait_send()

    voc_load.wait()
    bias_load.wait()
    if relay:
        last = passages - 1
        arrive(0)
        arrive(1)

        @pl.loop(0, passages // 2)
        def _(i):
            for q in range(2):
                forward(2 * i + q, 0).wait_recv()
            score([(0, s, 2 * i + q) for s in range(2) for q in range(2)])

        @pl.loop(0, passages)
        def _(p):
            @pl.when((p > 0) & (p < last))
            def _():
                arrive(p + 1)

            @pl.when(p == 1)
            def _():
                exchange_groups()

            for k in (1, 2):
                forward(p, k).wait_recv()
            score([(k, s, p) for k in (1, 2) for s in range(2)])

        arrive_far(0)

        @pl.loop(0, passages)
        def _(p):
            @pl.when(p == 0)
            def _():
                exchange_cores()

            @pl.when(p == 1)
            def _():
                place()

            @pl.when(p < last)
            def _():
                arrive_far(p + 1)

            @pl.when(p == last)
            def _():
                settle()

            forward(p, 3).wait_recv()
            score([(3, s, p) for s in range(2)])

        forward(last, 3).wait_send()
    else:
        exchange_groups()

        @pl.loop(1, chips)
        def _(k):
            @pl.loop(0, passages)
            def _(p):
                tok_copy(p, k).wait_recv()
                forward(p, k).start()

        exchange_cores()

        @pl.loop(0, chips)
        def _(k):
            @pl.loop(0, passages)
            def _(p):
                forward(p, k).wait_recv()
                score([(k, s, p) for s in range(2)])

        place()
        settle()

    raw = res[...] + bias[...].astype(F32)[None, :]
    sparse_out[...] = jnp.where(mask[...] > 0.5, jnp.log1p(jnp.maximum(raw, 0.0)), 0.0).astype(BF16)


def finish(a_ref, b_ref, c_ref, a_out, b_out, c_out):
    a_out[...] = a_ref[...]
    b_out[...] = b_ref[...]
    c_out[...] = c_ref[...]


def body(
    groups,
    n,
    hidden,
    lengths,
    block_list,
    cluster_ids,
    attn_weight,
    out_weight,
    up_weight,
    down_weight,
    head_weight,
    head_gain,
    vocab_weight,
    vocab_bias,
    centroids,
):
    passages = lengths.shape[0]
    tokens, width = hidden.shape
    seq = tokens // passages
    ff = up_weight.shape[1]
    terms = vocab_weight.shape[0]
    devices = groups * n
    chips = n // 2
    side = math.isqrt(chips)
    chunk_passages = 1
    chunks = passages // chunk_passages
    rows = chunk_passages * seq
    packed = width // 2 + max(n * terms // BLOCK, 128)
    vm = pl.BlockSpec(memory_space=pltpu.VMEM)
    hbm = pl.BlockSpec(memory_space=pl.ANY)
    dma = pltpu.SemaphoreType.DMA
    operands = (
        hidden,
        lengths,
        block_list,
        cluster_ids,
        attn_weight,
        out_weight,
        up_weight,
        down_weight,
        head_weight,
        head_gain,
        vocab_weight,
        vocab_bias,
        centroids,
    )
    local = [
        (pltpu.SMEM if x is lengths or x is cluster_ids else pltpu.VMEM)(x.shape, x.dtype)
        for x in operands
    ]
    found = pl.pallas_call(
        functools.partial(kernel, groups, n, side, seq, chunk_passages),
        out_shape=(
            jax.ShapeDtypeStruct((n * passages, terms), BF16),
            jax.ShapeDtypeStruct((1, CAP, width), BF16),
            jax.ShapeDtypeStruct((1, CAP), jnp.int32),
        ),
        in_specs=[hbm] * 13,
        out_specs=(vm, vm, vm),
        scratch_shapes=local
        + [
            pltpu.VMEM((chips, 2, tokens, width), BF16),
            pltpu.VMEM((rows, 3 * width), BF16),
            pltpu.VMEM((rows, width), BF16),
            pltpu.VMEM((rows, width), BF16),
            pltpu.VMEM((rows, ff), BF16),
            pltpu.VMEM((2 * passages, packed), F32),
            pltpu.VMEM((2 * passages, packed), BF16),
            pltpu.VMEM((2, groups, chips, 2 * passages, packed), BF16),
            pltpu.VMEM((n * passages, terms), F32),
            pltpu.VMEM((n * passages, terms), F32),
            dma((chunks + 15,)),
            dma((passages, chips + 1)),
            dma((passages, chips + 1)),
            dma((passages, chips)),
            dma((passages, chips)),
            dma((chips,)),
            dma((chips,)),
            dma((groups,)),
            dma((groups,)),
            dma((1,)),
            dma((1,)),
        ],
        compiler_params=pltpu.CompilerParams(
            collective_id=0, has_side_effects=True, vmem_limit_bytes=60 * 1024 * 1024
        ),
    )(*operands)
    return pl.pallas_call(
        finish,
        out_shape=tuple(jax.ShapeDtypeStruct(f.shape, f.dtype) for f in found),
        in_specs=[vm] * 3,
        out_specs=(vm,) * 3,
    )(*found)


def solution(mesh):
    placed = (
        P(("grp", "term"), None),
        P(("grp", "term")),
        P(("grp", "term"), None),
        P(("grp", "term")),
        P(),
        P(),
        P(),
        P(),
        P(),
        P(),
        P("term", None),
        P("term"),
        P(("grp", "term"), None),
    )
    return jax.shard_map(
        functools.partial(body, mesh.shape["grp"], mesh.shape["term"]),
        mesh=mesh,
        in_specs=placed,
        out_specs=(P("grp", "term"), P(("grp", "term"), None, None), P(("grp", "term"), None)),
        check_vma=False,
    )
```

```python
import functools
import math

import jax
import jax.numpy as jnp
from jax import lax
from jax.experimental import pallas as pl
from jax.experimental.pallas import tpu as pltpu
from jax.sharding import PartitionSpec as P

HEAD = 64
BLOCK = 128
CL_DEV = 512
CAP = 16
MESH = pl.DeviceIdType.MESH
F32 = jnp.float32
BF16 = jnp.bfloat16


def norm(values):
    center = values - jnp.mean(values, axis=-1, keepdims=True)
    spread = jnp.mean(center * center, axis=-1, keepdims=True)
    return center * lax.rsqrt(spread + 1e-06)


def gelu(v):
    return (0.5 * v) * (1.0 + lax.erf(v * math.sqrt(0.5)))


def mm(a, b):
    return jnp.dot(a, b, preferred_element_type=F32)


def mm_nt(a, b):
    return lax.dot_general(a, b, (((1,), (1,)), ((), ())), preferred_element_type=F32)


def kernel(
    groups,
    n,
    side,
    seq,
    chunk_passages,
    hid_hbm,
    len_hbm,
    blk_hbm,
    cid_hbm,
    aw_hbm,
    ow_hbm,
    uw_hbm,
    dw_hbm,
    hw_hbm,
    gain_hbm,
    voc_hbm,
    bias_hbm,
    cen_hbm,
    sparse_out,
    dense_out,
    slot_out,
    hid,
    len_ref,
    blk,
    cid_ref,
    aw,
    ow,
    uw,
    dw,
    hw,
    gain,
    voc,
    bias,
    cen,
    gath,
    joined,
    ctx,
    fst,
    inner,
    dacc,
    payload,
    dall,
    res,
    mask,
    wsem,
    tok_send,
    tok_recv,
    f_send,
    f_recv,
    d_send,
    d_recv,
    z_send,
    z_recv,
    x_send,
    x_recv,
):
    grp = lax.axis_index("grp")
    term = lax.axis_index("term")
    devices = groups * n
    me = grp * n + term
    chips = n // 2
    chip = term // 2
    core = term % 2
    partner = {"grp": grp, "term": chip * 2 + (1 - core)}
    cy, cx = chip // side, chip % side
    width = hid.shape[1]
    rows = chunk_passages * seq
    passages = len_ref.shape[0]
    chunks = passages // chunk_passages
    ff = uw.shape[1]
    relay = side == 2
    cut = seq // 2
    split = width // 2
    tile = ff // 2

    def other(k):
        ky, kx = k // side, k % side
        to = ((cy + ky) % side) * side + (cx + kx) % side
        return {"grp": grp, "term": to * 2 + core}

    def source(k):
        ky, kx = k // side, k % side
        return ((cy + side - ky) % side) * side + (cx + side - kx) % side

    def everyone(d):
        to = (me + d) % devices
        return {"grp": to // n, "term": to % n}

    def load(i, src, dst):
        return pltpu.make_async_copy(src, dst, wsem.at[i])

    def hid_load(h):
        span = pl.ds(pl.multiple_of(h * rows, rows), rows)
        return load(h, hid_hbm.at[span], hid.at[span])

    def aw_load(c):
        cols = pl.ds(c * width, width)
        return load(chunks + c, aw_hbm.at[:, cols], aw.at[:, cols])

    def uw_load(j):
        cols = pl.ds(pl.multiple_of(j * tile, tile), tile)
        return load(chunks + 3 + j, uw_hbm.at[:, cols], uw.at[:, cols])

    base = chunks + 5
    ow_load = load(base, ow_hbm, ow)
    dw_load = load(base + 1, dw_hbm, dw)
    hw_load = load(base + 2, hw_hbm, hw)
    voc_load = load(base + 3, voc_hbm, voc)
    cen_load = load(base + 4, cen_hbm, cen)
    gain_load = load(base + 5, gain_hbm, gain)
    bias_load = load(base + 6, bias_hbm, bias)
    blk_load = load(base + 7, blk_hbm, blk)
    len_load = load(base + 8, len_hbm, len_ref)
    cid_load = load(base + 9, cid_hbm, cid_ref)

    len_load.start()
    hid_load(0).start()
    for c in range(3):
        aw_load(c).start()
    ow_load.start()

    barrier = pltpu.get_barrier_semaphore()

    @pl.loop(1, devices)
    def _(d):
        pl.semaphore_signal(barrier, inc=1, device_id=everyone(d), device_id_type=MESH)

    def seat(p):
        return pl.ds(pl.multiple_of(p * seq, seq), seq)

    def tok_copy(p, k):
        return pltpu.make_async_remote_copy(
            src_ref=gath.at[0, 0, seat(p)],
            dst_ref=gath.at[k, 0, seat(p)],
            send_sem=tok_send.at[p, k],
            recv_sem=tok_recv.at[p, k],
            device_id=other(k),
            device_id_type=MESH,
        )

    def relay_copy(p, part):
        via = 1 + part
        start, size = ((0, cut), (cut, seq - cut))[part]
        span = pl.ds(pl.multiple_of(p * seq + start, 16), size)
        return pltpu.make_async_remote_copy(
            src_ref=gath.at[via, 0, span],
            dst_ref=gath.at[3, 0, span],
            send_sem=tok_send.at[p, 3 + part],
            recv_sem=tok_recv.at[p, 3 + part],
            device_id=other(2 - part),
            device_id_type=MESH,
        )

    def forward(p, k):
        return pltpu.make_async_remote_copy(
            src_ref=gath.at[k, 0, seat(p)],
            dst_ref=gath.at[k, 1, seat(p)],
            send_sem=f_send.at[p, k],
            recv_sem=f_recv.at[p, k],
            device_id=partner,
            device_id_type=MESH,
        )

    def far_forward(p, part):
        span = pl.ds(pl.multiple_of(p * seq + part * cut, 16), cut)
        return pltpu.make_async_remote_copy(
            src_ref=gath.at[3, 0, span],
            dst_ref=gath.at[3, 1, span],
            send_sem=f_send.at[p, 3 + part],
            recv_sem=f_recv.at[p, 3 + part],
            device_id=partner,
            device_id_type=MESH,
        )

    def plane_copy(k):
        return pltpu.make_async_remote_copy(
            src_ref=payload,
            dst_ref=dall.at[0, grp, chip],
            send_sem=d_send.at[k],
            recv_sem=d_recv.at[k],
            device_id=other(k),
            device_id_type=MESH,
        )

    def group_copy(j):
        return pltpu.make_async_remote_copy(
            src_ref=dall.at[0, grp],
            dst_ref=dall.at[0, grp],
            send_sem=z_send.at[j],
            recv_sem=z_recv.at[j],
            device_id={"grp": (grp + j) % groups, "term": term},
            device_id_type=MESH,
        )

    dense_forward = pltpu.make_async_remote_copy(
        src_ref=dall.at[0],
        dst_ref=dall.at[1],
        send_sem=x_send.at[0],
        recv_sem=x_recv.at[0],
        device_id=partner,
        device_id_type=MESH,
    )

    def send_direct(p):
        if relay:
            tok_copy(p, 1).start()
            tok_copy(p, 2).start()
        else:

            @pl.loop(1, chips)
            def _(k):
                tok_copy(p, k).start()

    listing = blk.shape[1]
    terms = voc_hbm.shape[0]
    blocks = n * terms // BLOCK
    pairs = width // (2 * HEAD)
    low = lax.broadcasted_iota(jnp.int32, (seq, 2 * HEAD), 1) < HEAD
    key_place = lax.broadcasted_iota(jnp.int32, (seq, 2 * seq), 0)
    upper = lax.broadcasted_iota(jnp.int32, (2 * HEAD, seq), 0) < HEAD
    row_place = lax.broadcasted_iota(jnp.int32, (seq, width), 0)

    def mark():
        blk_load.wait()
        cid_load.wait()
        dacc[:, split:] = jnp.zeros_like(dacc[:, split:])
        square = lax.broadcasted_iota(jnp.int32, (listing, listing), 0) == lax.broadcasted_iota(
            jnp.int32, (listing, listing), 1
        )
        block_lane = lax.broadcasted_iota(jnp.int32, (listing, blocks), 1).astype(F32)
        id_lane = lax.broadcasted_iota(jnp.int32, (1, 128), 1)
        for p in range(passages):
            line = blk[p : p + 1, :].astype(F32)
            column = jnp.sum(jnp.where(square, line, 0.0), axis=1, keepdims=True)
            marks = jnp.max(jnp.where(column == block_lane, 1.0, 0.0), axis=0, keepdims=True)
            dacc[p : p + 1, split : split + blocks] = marks
            cid = cid_ref[p]
            ids = jnp.where(id_lane == 0, cid // 256, jnp.where(id_lane == 1, cid % 256, 0))
            dacc[passages + p : passages + p + 1, split : split + 128] = ids.astype(F32)

    def attend(i, live):
        span = slice(i * seq, (i + 1) * seq)
        for pair in range(pairs):
            at = pair * 2 * HEAD
            q = joined[span, at : at + 2 * HEAD]
            k = joined[span, width + at : width + at + 2 * HEAD]
            v = joined[span, 2 * width + at : 2 * width + at + 2 * HEAD]
            zero = jnp.zeros_like(q)
            both = jnp.concatenate([jnp.where(low, q, zero), jnp.where(low, zero, q)], axis=0)
            scores = jnp.where(live, mm_nt(k, both), -1e30)
            top = jnp.max(scores, axis=0, keepdims=True)
            expo = jnp.exp2((scores - top) * (math.log2(math.e) / math.sqrt(HEAD)))
            scale = 1.0 / jnp.sum(expo, axis=0, keepdims=True)
            mixed = mm(v.T, expo.astype(BF16)) * scale
            ctx[span, at : at + 2 * HEAD] = jnp.where(upper, mixed[:, :seq], mixed[:, seq:]).astype(BF16).T

    def arrive(p):
        for part in range(2):
            tok_copy(p, 1 + part).wait_recv()
            relay_copy(p, part).start()
        for part in range(2):
            forward(p, 1 + part).start()

    def arrive_far(p):
        for part in range(2):
            relay_copy(p, part).wait_recv()
            far_forward(p, part).start()

    def encode(h):
        hid_load(h).wait()
        if h == 0:
            aw_load(0).wait()
            for j in range(2):
                uw_load(j).start()
            dw_load.start()
            hw_load.start()
            gain_load.start()
        x = hid[h * rows : (h + 1) * rows, :]
        for c in range(3):
            if h == 0 and c > 0:
                aw_load(c).wait()
            cols = slice(c * width, (c + 1) * width)
            joined[:, cols] = mm(x, aw[:, cols]).astype(BF16)
        if h == 0:
            len_load.wait()
            for i in range(1, chunks):
                hid_load(i).start()
            voc_load.start()
            bias_load.start()
            blk_load.start()
            cid_load.start()
            cen_load.start()
        limits = [len_ref[h * chunk_passages + i] for i in range(chunk_passages)]
        for i in range(chunk_passages):
            attend(i, key_place < limits[i])
        if h == 0:
            ow_load.wait()
        fst[...] = norm(x.astype(F32) + mm(ctx[...], ow[...])).astype(BF16)
        if h == 0:
            for j in range(2):
                uw_load(j).wait()
        inner[...] = gelu(mm(fst[...], uw[...])).astype(BF16)
        if h == 0:
            dw_load.wait()
        layer_out = norm(fst[...].astype(F32) + mm(inner[...], dw[...])).astype(BF16)
        wide = layer_out.astype(F32)
        for i in range(chunk_passages):
            p = h * chunk_passages + i
            dacc[p : p + 1, 0:split] = wide[i * seq : i * seq + 1, :split]
            dacc[passages + p : passages + p + 1, 0:split] = wide[i * seq : i * seq + 1, split:]
        if h == 0:
            pl.semaphore_wait(barrier, devices - 1)
        if h == chunks - 1:
            mark()
            payload[...] = dacc[...].astype(BF16)
            dall[0, grp, chip] = payload[...]

            @pl.loop(1, chips)
            def _(k):
                plane_copy(k).start()

        if h == 0:
            hw_load.wait()
            gain_load.wait()
        out = norm(gelu(mm(layer_out, hw[...]))) * gain[...][None, :]
        for i in range(chunk_passages):
            p = h * chunk_passages + i
            one = out[i * seq : (i + 1) * seq]
            one = jnp.where(row_place < limits[i], one, one[0:1])
            gath[0, 0, p * seq : (p + 1) * seq, :] = one.astype(BF16)
            send_direct(p)
        for i in range(chunk_passages):
            forward(h * chunk_passages + i, 0).start()

    for h in range(chunks):
        encode(h)

    wide_tile = min(2048, terms)

    def score(seats):
        spot = []
        for k, s, p in seats:
            c = source(k)
            cc = core if s == 0 else 1 - core
            spot.append((c * 2 + cc) * passages + p)

        for j in range(terms // wide_tile):
            cols = slice(j * wide_tile, (j + 1) * wide_tile)
            lhs = jnp.concatenate([gath[k, s, seat(p), :] for k, s, p in seats], axis=0)
            logits = mm_nt(lhs, voc[cols, :])
            for i, at in enumerate(spot):
                res[pl.ds(at, 1), cols] = jnp.max(
                    logits[i * seq : (i + 1) * seq], axis=0, keepdims=True
                )

    def exchange_groups():
        @pl.loop(1, chips)
        def _(k):
            plane_copy(k).wait_recv()

        @pl.loop(1, groups)
        def _(j):
            group_copy(j).start()

    def exchange_cores():
        @pl.loop(1, groups)
        def _(j):
            group_copy(j).wait_recv()

        dense_forward.start()

    def place():
        dense_forward.wait_recv()
        cen_load.wait()
        span = 2 * passages
        total = devices * span
        flat = dall[...].astype(F32).reshape(total, dall.shape[-1])
        facts = flat[:, split : split + 128].astype(BF16)
        pick = lax.broadcasted_iota(jnp.int32, (8, 128), 0) == lax.broadcasted_iota(
            jnp.int32, (8, 128), 1
        )
        pieces = pltpu.roll(
            mm_nt(jnp.where(pick, 1.0, 0.0).astype(BF16), facts), total - passages, 1
        )
        clusters = pieces[0:1] * 256.0 + pieces[1:2]

        def numbered(shape, axis):
            place = lax.broadcasted_iota(jnp.int32, shape, axis)
            sender, within = place // span, place % span
            stream, spot = sender // (groups * chips), sender % (groups * chips)
            cc = jnp.where(stream == 0, core, 1 - core)
            return (spot * 2 + cc) * passages + within, within

        passage, within = numbered((1, total), 1)
        above, _ = numbered((total, 1), 0)
        first = (me * CL_DEV).astype(F32)
        local = clusters - first
        own = (within < passages) & (local >= 0.0) & (local < CL_DEV)
        own = jnp.where(own, 1.0, 0.0)
        before = above < passage
        ranks = mm(
            jnp.broadcast_to(own, (8, total)).astype(BF16), jnp.where(before, 1.0, 0.0).astype(BF16)
        )[0:1]
        slot = lax.broadcasted_iota(jnp.int32, (CAP, total), 0).astype(F32)
        chosen = jnp.where((slot == ranks) & (own > 0.5), 1.0, 0.0)
        filled = jnp.sum(chosen, axis=1, keepdims=True) > 0.5
        number = jnp.sum(chosen * (passage.astype(F32) + 1.0), axis=1, keepdims=True) - 1.0
        local = jnp.where(own > 0.5, local, 0.0)
        entry = jnp.sum(chosen * local, axis=1, keepdims=True)
        both = jnp.concatenate([chosen, pltpu.roll(chosen, passages, 1)], axis=0).astype(BF16)
        picked = mm(both, flat[:, :split].astype(BF16))
        entries = lax.broadcasted_iota(jnp.int32, (CAP, CL_DEV), 1).astype(F32)
        lookup = jnp.where((entries == entry) & filled, 1.0, 0.0).astype(BF16)
        for part in range(2):
            cols = slice(part * split, (part + 1) * split)
            dense_out[0, :, cols] = jnp.where(
                filled, picked[part * CAP : (part + 1) * CAP] - mm(lookup, cen[:, cols]), 0.0
            ).astype(BF16)
        eye = lax.broadcasted_iota(jnp.int32, (CAP, CAP), 0) == lax.broadcasted_iota(
            jnp.int32, (CAP, CAP), 1
        )
        slot_out[...] = jnp.sum(jnp.where(eye, number, 0.0), axis=0, keepdims=True).astype(
            jnp.int32
        )
        marks = []
        for c in range(chips):
            for s in (core, 1 - core):
                marks.append(dall[s, grp, c, :, split : split + blocks].astype(F32)[:passages])
        marks = jnp.concatenate(marks, axis=0).astype(BF16)
        lead = term * (terms // BLOCK)
        offset = (lax.broadcasted_iota(jnp.int32, (blocks, terms), 0) - lead) * BLOCK
        column = lax.broadcasted_iota(jnp.int32, (blocks, terms), 1)
        spread = jnp.where((column >= offset) & (column < offset + BLOCK), 1.0, 0.0).astype(BF16)
        mask[...] = mm(marks, spread)

    def settle():
        @pl.loop(1, chips)
        def _(k):
            plane_copy(k).wait_send()

        @pl.loop(1, groups)
        def _(j):
            group_copy(j).wait_send()

        dense_forward.wait_send()

        @pl.loop(0, passages)
        def _(p):
            @pl.loop(0, chips - 1 if relay else chips)
            def _(k):
                forward(p, k).wait_send()

            if relay:
                for part in range(2):
                    tok_copy(p, 1 + part).wait_send()
                    relay_copy(p, part).wait_send()
            else:

                @pl.loop(1, chips)
                def _(k):
                    tok_copy(p, k).wait_send()

        if relay:

            @pl.loop(0, passages - 1)
            def _(p):
                for part in range(2):
                    far_forward(p, part).wait_send()

    voc_load.wait()
    bias_load.wait()
    if relay:
        last = passages - 1
        arrive(0)
        arrive(1)

        @pl.loop(0, passages // 2)
        def _(i):
            for q in range(2):
                forward(2 * i + q, 0).wait_recv()
            score([(0, s, 2 * i + q) for s in range(2) for q in range(2)])

        @pl.loop(0, passages)
        def _(p):
            @pl.when((p > 0) & (p < last))
            def _():
                arrive(p + 1)

            @pl.when(p == 1)
            def _():
                exchange_groups()

            for k in (1, 2):
                forward(p, k).wait_recv()
            score([(k, s, p) for k in (1, 2) for s in range(2)])

        arrive_far(0)

        @pl.loop(0, passages)
        def _(p):
            @pl.when(p == 0)
            def _():
                exchange_cores()

            @pl.when(p == 1)
            def _():
                place()

            @pl.when(p < last)
            def _():
                arrive_far(p + 1)

            @pl.when(p == last)
            def _():
                settle()

            for part in range(2):
                far_forward(p, part).wait_recv()
            score([(3, s, p) for s in range(2)])

        for part in range(2):
            far_forward(last, part).wait_send()
    else:
        exchange_groups()

        @pl.loop(1, chips)
        def _(k):
            @pl.loop(0, passages)
            def _(p):
                tok_copy(p, k).wait_recv()
                forward(p, k).start()

        exchange_cores()

        @pl.loop(0, chips)
        def _(k):
            @pl.loop(0, passages)
            def _(p):
                forward(p, k).wait_recv()
                score([(k, s, p) for s in range(2)])

        place()
        settle()

    raw = res[...] + bias[...].astype(F32)[None, :]
    sparse_out[...] = jnp.where(mask[...] > 0.5, jnp.log1p(jnp.maximum(raw, 0.0)), 0.0).astype(BF16)


def finish(a_ref, b_ref, c_ref, a_out, b_out, c_out):
    a_out[...] = a_ref[...]
    b_out[...] = b_ref[...]
    c_out[...] = c_ref[...]


def body(
    groups,
    n,
    hidden,
    lengths,
    block_list,
    cluster_ids,
    attn_weight,
    out_weight,
    up_weight,
    down_weight,
    head_weight,
    head_gain,
    vocab_weight,
    vocab_bias,
    centroids,
):
    passages = lengths.shape[0]
    tokens, width = hidden.shape
    seq = tokens // passages
    ff = up_weight.shape[1]
    terms = vocab_weight.shape[0]
    devices = groups * n
    chips = n // 2
    side = math.isqrt(chips)
    chunk_passages = 1
    chunks = passages // chunk_passages
    rows = chunk_passages * seq
    packed = width // 2 + max(n * terms // BLOCK, 128)
    vm = pl.BlockSpec(memory_space=pltpu.VMEM)
    hbm = pl.BlockSpec(memory_space=pl.ANY)
    dma = pltpu.SemaphoreType.DMA
    operands = (
        hidden,
        lengths,
        block_list,
        cluster_ids,
        attn_weight,
        out_weight,
        up_weight,
        down_weight,
        head_weight,
        head_gain,
        vocab_weight,
        vocab_bias,
        centroids,
    )
    local = [
        (pltpu.SMEM if x is lengths or x is cluster_ids else pltpu.VMEM)(x.shape, x.dtype)
        for x in operands
    ]
    found = pl.pallas_call(
        functools.partial(kernel, groups, n, side, seq, chunk_passages),
        out_shape=(
            jax.ShapeDtypeStruct((n * passages, terms), BF16),
            jax.ShapeDtypeStruct((1, CAP, width), BF16),
            jax.ShapeDtypeStruct((1, CAP), jnp.int32),
        ),
        in_specs=[hbm] * 13,
        out_specs=(vm, vm, vm),
        scratch_shapes=local
        + [
            pltpu.VMEM((chips, 2, tokens, width), BF16),
            pltpu.VMEM((rows, 3 * width), BF16),
            pltpu.VMEM((rows, width), BF16),
            pltpu.VMEM((rows, width), BF16),
            pltpu.VMEM((rows, ff), BF16),
            pltpu.VMEM((2 * passages, packed), F32),
            pltpu.VMEM((2 * passages, packed), BF16),
            pltpu.VMEM((2, groups, chips, 2 * passages, packed), BF16),
            pltpu.VMEM((n * passages, terms), F32),
            pltpu.VMEM((n * passages, terms), F32),
            dma((chunks + 15,)),
            dma((passages, chips + 1)),
            dma((passages, chips + 1)),
            dma((passages, chips + 1)),
            dma((passages, chips + 1)),
            dma((chips,)),
            dma((chips,)),
            dma((groups,)),
            dma((groups,)),
            dma((1,)),
            dma((1,)),
        ],
        compiler_params=pltpu.CompilerParams(
            collective_id=0, has_side_effects=True, vmem_limit_bytes=60 * 1024 * 1024
        ),
    )(*operands)
    return pl.pallas_call(
        finish,
        out_shape=tuple(jax.ShapeDtypeStruct(f.shape, f.dtype) for f in found),
        in_specs=[vm] * 3,
        out_specs=(vm,) * 3,
    )(*found)


def solution(mesh):
    placed = (
        P(("grp", "term"), None),
        P(("grp", "term")),
        P(("grp", "term"), None),
        P(("grp", "term")),
        P(),
        P(),
        P(),
        P(),
        P(),
        P(),
        P("term", None),
        P("term"),
        P(("grp", "term"), None),
    )
    return jax.shard_map(
        functools.partial(body, mesh.shape["grp"], mesh.shape["term"]),
        mesh=mesh,
        in_specs=placed,
        out_specs=(P("grp", "term"), P(("grp", "term"), None, None), P(("grp", "term"), None)),
        check_vma=False,
    )
```
